32 devices in a mesh: rep: 8 (over y, x, core), shard: 4 (over z).
Axes of the slice: x: 2, y: 2, z: 4, core: 2. Of those that a mesh axis runs over, the one named last changes fastest.
Arguments:
- layer_input: bfloat16 [4096, 1024], P(('rep', 'shard')), may hold values from -6 to 6
- segment_ids: int32 [4096], P(('rep', 'shard')), may hold values from -1 to 127, as said below
- cotangent: bfloat16 [4096, 1024], P(('rep', 'shard')), may hold values from -16 to 16
- norm_gain: float32 [1024], replicated, may hold values from 0.5 to 1.5
- w_query: bfloat16 [1024, 512], P('shard'), may hold values from -3 to 3
- key_value_weight: bfloat16 [1024, 256], P('shard'), may hold values from -0.1875 to 0.1875
- w_mixer_in: bfloat16 [1024, 3352], P('shard'), may hold values from -0.1875 to 0.1875
- conv_weight: float32 [4, 1792], replicated, may hold values from -3 to 3
- conv_bias: float32 [1792], replicated, may hold values from -3 to 3
- dt_bias: float32 [24], replicated, may hold values from -3 to 0
- decay_log: float32 [24], replicated, may hold values from -4.6 to 0
- skip_gain: float32 [24], replicated, may hold values from 0.5 to 1.5
- mixer_gain: float32 [1536], replicated, may hold values from 0.5 to 1.5
- w_mixer_out: bfloat16 [1536, 1024], P('shard'), may hold values from -0.15625 to 0.15625
- w_attn_out: bfloat16 [512, 1024], P('shard'), may hold values from -0.75 to 0.75
- ffn_gain: float32 [1024], replicated, may hold values from 0.5 to 1.5
- w_gate_up: bfloat16 [1024, 4096], P('shard'), may hold values from -0.1875 to 0.1875
- w_down: bfloat16 [2048, 1024], P('shard'), may hold values from -0.125 to 0.125
Outputs:
- layer_output: bfloat16 [4096, 1024], P(('rep', 'shard'))
- grad_input: float32 [4096, 1024], P(('rep', 'shard'))
- grad_norm_gain: float32 [1024], replicated
- grad_w_query: float32 [1024, 512], P('shard')
- grad_w_keyval: float32 [1024, 256], P('shard')
- grad_w_mixer_in: float32 [1024, 3352], P('shard')
- grad_conv_weight: float32 [4, 1792], replicated
- grad_conv_bias: float32 [1792], replicated
- grad_dt_bias: float32 [24], replicated
- grad_decay_log: float32 [24], replicated
- grad_skip_gain: float32 [24], replicated
- grad_mixer_gain: float32 [1536], replicated
- grad_w_mixer_out: float32 [1536, 1024], P('shard')
- grad_w_attn_out: float32 [512, 1024], P('shard')
- grad_ffn_gain: float32 [1024], replicated
- grad_w_gate_up: float32 [1024, 4096], P('shard')
- grad_w_down: float32 [2048, 1024], P('shard')
The draws below stay inside these ranges and needn't reach their ends.
Inputs may be any that keep to these rules, and one draw needn't show every extreme that they name: `segment_ids`: -1 marks padding slots, which follow the live slots within each device's 128 slots; live slots carry 0, 1, 2, ... from each device's first slot, one number a segment, so no segment crosses a device's slots; some device has all slots live and some only 32.
All inputs are finite; a program needn't handle non-finite values.
Results may differ from the reference program's by a relative error of at most 0.017.
The reference program's roundings to bfloat16 on the way count: a program that leaves them out, or rounds other values in their place, can miss the bound.
Values may be sent and summed in bfloat16 or wider, within the bound.
No kernel may reach another device: no remote copies, remote signals or barrier semaphores. Data moves between devices by JAX's collectives and lax.ppermute only.
A program may use at most 192 MiB of HBM per device.

```python
import math
import jax
import jax.numpy as jnp
from jax import lax

MODEL_WIDTH = 1024
FF = 2048
MH = 24
HEAD_SIZE = 64
NS = 128
KC = 4
QUERY_HEADS = 8
KEY_VALUE_HEADS = 2
TOK_DEV = 128
DI = 1536
ATT = 512
CONV = 1792
IN_COLS = 3352
TOKENS = 4096


def draw_segment_ids(key, part):
    tile_count = TOKENS // TOK_DEV
    key_live = jax.random.fold_in(key, 11)
    key_break = jax.random.fold_in(key, 12)
    live_count = jax.random.randint(key_live, (tile_count,), TOK_DEV // 4, TOK_DEV + 1)
    live_count = live_count.at[0].set(TOK_DEV).at[tile_count - 1].set(TOK_DEV // 4)
    breaks = (jax.random.randint(key_break, (tile_count, TOK_DEV), 0, 24) == 0).astype(jnp.int32)
    breaks = breaks.at[:, 0].set(1).at[0, :].set(1)
    numbers = jnp.cumsum(breaks, axis=1) - 1
    offsets = jnp.arange(TOK_DEV, dtype=jnp.int32)[None, :]
    return jnp.where(offsets < live_count[:, None], numbers, -1).reshape(TOKENS).astype(jnp.int32)


def draw_cotangent(key, part):
    ramp = (jnp.arange(TOKENS, dtype=jnp.float32) / TOKENS)[:, None]
    values = jnp.clip(jax.random.normal(key, (TOKENS, MODEL_WIDTH), jnp.float32), -5.0, 5.0) * 3.0 ** ramp
    return values.astype(jnp.bfloat16)


def draw_w_query(key, part):
    values = jnp.clip(jax.random.normal(key, (MODEL_WIDTH, QUERY_HEADS * HEAD_SIZE), jnp.float32), -6.0, 6.0) / MODEL_WIDTH ** 0.5
    return values.astype(jnp.bfloat16)


def shard_levels(key, dims, pieces, smallest, high):
    loudness = 1.0
    for axis_at, parts in pieces:
        draws = jax.random.uniform(jax.random.fold_in(jax.random.fold_in(key, 6), axis_at), (parts,), jnp.float32, smallest / len(pieces), high / len(pieces))
        loudness = loudness * jnp.repeat(jnp.exp(draws), dims[axis_at] // parts).reshape((-1,) + (1,) * (len(dims) - 1 - axis_at))
    return loudness


def normal_values(rng, dims, spread, most, shards=(), kind=jnp.bfloat16):
    drawn = jax.random.normal(rng, dims, jnp.float32) * spread
    if len(shards) > 0:
        drawn = shard_levels(rng, dims, shards, -0.22, 0.18) * drawn
    return jnp.clip(drawn, min=-most, max=most).astype(kind)


def setup_inputs(seed: int = 0) -> dict:
    key_of = jax.random.split(jax.random.key(seed), 19)
    layer_input = normal_values(key_of[0], (TOKENS, MODEL_WIDTH), 1.0, 6.0, ((0, 32),))
    segment_ids = draw_segment_ids(jax.random.fold_in(key_of[18], 71), 0)
    cotangent = draw_cotangent(jax.random.fold_in(key_of[18], 71), 0)
    norm_gain = jnp.clip(1.0 + 0.1 * jax.random.normal(key_of[3], (MODEL_WIDTH,), jnp.float32), 0.5, 1.5)
    w_query = draw_w_query(jax.random.fold_in(key_of[18], 71), 0)
    key_value_weight = normal_values(key_of[5], (MODEL_WIDTH, 2 * KEY_VALUE_HEADS * HEAD_SIZE), MODEL_WIDTH ** -0.5, 0.1875, ((0, 4),))
    w_mixer_in = normal_values(key_of[6], (MODEL_WIDTH, IN_COLS), MODEL_WIDTH ** -0.5, 0.1875, ((0, 4),))
    conv_weight = normal_values(key_of[7], (KC, CONV), 0.5, 3.0, (), jnp.float32)
    conv_bias = normal_values(key_of[8], (CONV,), 0.5, 3.0, (), jnp.float32)
    dt_bias = jnp.clip(jax.random.uniform(key_of[9], (MH,), jnp.float32, -3.0, 0.0), -3.0, 0.0)
    decay_log = jnp.clip(jax.random.uniform(key_of[10], (MH,), jnp.float32, -4.6, 0.0), -4.6, 0.0)
    skip_gain = jnp.clip(jax.random.uniform(key_of[11], (MH,), jnp.float32, 0.5, 1.5), 0.5, 1.5)
    mixer_gain = jnp.clip(1.0 + 0.1 * jax.random.normal(key_of[12], (DI,), jnp.float32), 0.5, 1.5)
    w_mixer_out = normal_values(key_of[13], (DI, MODEL_WIDTH), DI ** -0.5, 0.15625, ((0, 4),))
    w_attn_out = normal_values(key_of[14], (ATT, MODEL_WIDTH), HEAD_SIZE ** -0.5, 0.75, ((0, 4),))
    ffn_gain = jnp.clip(1.0 + 0.1 * jax.random.normal(key_of[15], (MODEL_WIDTH,), jnp.float32), 0.5, 1.5)
    w_gate_up = normal_values(key_of[16], (MODEL_WIDTH, 2 * FF), MODEL_WIDTH ** -0.5, 0.1875, ((0, 4),))
    w_down = normal_values(key_of[17], (FF, MODEL_WIDTH), FF ** -0.5, 0.125, ((0, 4),))
    return {"layer_input": layer_input, "segment_ids": segment_ids, "cotangent": cotangent, "norm_gain": norm_gain, "w_query": w_query, "key_value_weight": key_value_weight, "w_mixer_in": w_mixer_in, "conv_weight": conv_weight, "conv_bias": conv_bias, "dt_bias": dt_bias, "decay_log": decay_log, "skip_gain": skip_gain, "mixer_gain": mixer_gain, "w_mixer_out": w_mixer_out, "w_attn_out": w_attn_out, "ffn_gain": ffn_gain, "w_gate_up": w_gate_up, "w_down": w_down}


EPS = 1e-05
ROPE_BASE = 100000000000.0

def product(left, right):
    return jnp.dot(left, right, preferred_element_type=jnp.float32)

def product_tn(left, right):
    return lax.dot_general(left, right, (((0,), (0,)), ((), ())), preferred_element_type=jnp.float32)

def product_nt(left, right):
    return lax.dot_general(left, right, (((1,), (1,)), ((), ())), preferred_element_type=jnp.float32)

def rms_norm(values, gain):
    return values * lax.rsqrt(lax.optimization_barrier(jnp.mean(values * values, axis=-1, keepdims=True)) + EPS) * gain

def positions_of(segments):
    item_count = segments.shape[0]
    index = jnp.arange(item_count, dtype=jnp.int32)
    starts = jnp.concatenate([jnp.ones((1,), bool), segments[1:] != segments[:-1]])
    begin = lax.cummax(jnp.where(starts, index, 0).astype(jnp.int32), axis=0)
    return (index - begin).astype(jnp.int32)

def rotate(values, position):
    half = HEAD_SIZE // 2
    freqs = ROPE_BASE ** (-2.0 * jnp.arange(half, dtype=jnp.float32) / HEAD_SIZE)
    angles = position.astype(jnp.float32)[:, None] * freqs[None, :]
    cosine = jnp.cos(angles)[:, None, :]
    sine = jnp.sin(angles)[:, None, :]
    first = values[..., :half]
    second = values[..., half:]
    return jnp.concatenate([first * cosine - second * sine, second * cosine + first * sine], axis=-1)

def silu(values):
    return values / (1.0 + jnp.exp(-values))

def mixer_core(query, key_value, mixer_in, conv_weight, conv_bias, dt_bias, decay_log, skip_gain, mixer_gain, position, allowed, same_seg):
    item_count = query.shape[0]
    heads_q = query.reshape(item_count, QUERY_HEADS, HEAD_SIZE)
    paired_items = key_value.reshape(item_count, 2, KEY_VALUE_HEADS, HEAD_SIZE)
    keys = rotate(paired_items[:, 0], position)
    values = paired_items[:, 1]
    heads_q = rotate(heads_q, position)
    shard_group = QUERY_HEADS // KEY_VALUE_HEADS
    keys = jnp.repeat(keys, shard_group, axis=1)
    values = jnp.repeat(values, shard_group, axis=1)
    scores = jnp.einsum('thd,shd->hts', heads_q, keys, precision=lax.Precision.HIGHEST) / math.sqrt(HEAD_SIZE)
    scores = jnp.where(allowed[None], scores, -jnp.inf)
    highest = lax.optimization_barrier(jnp.max(scores, axis=-1, keepdims=True))
    expo = jnp.exp(scores - highest)
    probs = expo / lax.optimization_barrier(jnp.sum(expo, axis=-1, keepdims=True))
    attended = jnp.einsum('hts,shd->thd', probs, values, precision=lax.Precision.HIGHEST).reshape(item_count, QUERY_HEADS * HEAD_SIZE)
    gate_z = mixer_in[:, :DI]
    conv_in = mixer_in[:, DI:DI + CONV]
    dt_raw = mixer_in[:, DI + CONV:]
    total = jnp.zeros((item_count, CONV), jnp.float32) + conv_bias[None, :]
    for offset in range(KC):
        shifted = jnp.concatenate([jnp.zeros((offset, CONV), jnp.float32), conv_in[:item_count - offset]], axis=0)
        total = total + conv_weight[KC - 1 - offset][None, :] * shifted * same_seg[offset][:, None]
    conv_out = silu(total)
    inner = conv_out[:, :DI].reshape(item_count, MH, HEAD_SIZE)
    bmat = conv_out[:, DI:DI + NS]
    cmat = conv_out[:, DI + NS:]
    step = jax.nn.softplus(dt_raw + dt_bias[None, :])
    csum = jnp.cumsum(step * (-jnp.exp(decay_log))[None, :], axis=0)
    gaps = csum[:, None, :] - csum[None, :, :]
    decay = jnp.exp(jnp.where(allowed[:, :, None], gaps, -jnp.inf))
    gram = jnp.dot(cmat, bmat.T, precision=lax.Precision.HIGHEST)
    mixing = gram[:, :, None] * decay * step[None, :, :]
    outputs = jnp.einsum('tsh,shp->thp', mixing, inner, precision=lax.Precision.HIGHEST)
    outputs = outputs + skip_gain[None, :, None] * inner
    gated = outputs.reshape(item_count, DI) * silu(gate_z)
    return (attended, rms_norm(gated, mixer_gain))

def swiglu(gate_up):
    return silu(gate_up[:, :FF]) * gate_up[:, FF:]

def forward_pass(rows, segments, mix_weights, ffn_weights, params):
    w_query, key_value_weight, w_mixer_in, w_mixer_out, w_attn_out = mix_weights
    w_gate_up, w_down = ffn_weights
    norm_gain, conv_weight, conv_bias, dt_bias, decay_log, skip_gain, mixer_gain, ffn_gain = params
    item_count = rows.shape[0]
    index = jnp.arange(item_count, dtype=jnp.int32)
    live = (segments >= 0).astype(jnp.float32)[:, None]
    allowed = (segments[:, None] == segments[None, :]) & (index[:, None] >= index[None, :])
    position = positions_of(segments)
    same_seg = jnp.stack([jnp.concatenate([jnp.zeros((offset,), jnp.float32), (segments[offset:] == segments[:item_count - offset]).astype(jnp.float32)]) for offset in range(KC)])
    wide = rows.astype(jnp.float32)
    normed, pull_first = jax.vjp(rms_norm, wide, norm_gain)
    normed_b = normed.astype(jnp.bfloat16)
    query = product(normed_b, w_query)
    key_value = product(normed_b, key_value_weight)
    mixer_in = product(normed_b, w_mixer_in)

    def core(query, key_value, mixer_in, conv_weight, conv_bias, dt_bias, decay_log, skip_gain, mixer_gain):
        return mixer_core(query, key_value, mixer_in, conv_weight, conv_bias, dt_bias, decay_log, skip_gain, mixer_gain, position, allowed, same_seg)
    (attended, mixed), pull_core = jax.vjp(core, query, key_value, mixer_in, conv_weight, conv_bias, dt_bias, decay_log, skip_gain, mixer_gain)
    attended_b = attended.astype(jnp.bfloat16)
    mixed_b = mixed.astype(jnp.bfloat16)
    middle = wide + live * (product(attended_b, w_attn_out) + product(mixed_b, w_mixer_out))
    normed2, pull_second = jax.vjp(rms_norm, middle, ffn_gain)
    normed2_b = normed2.astype(jnp.bfloat16)
    gate_up = product(normed2_b, w_gate_up)
    act, pull_act = jax.vjp(swiglu, gate_up)
    act_b = act.astype(jnp.bfloat16)
    layer_output = (middle + live * product(act_b, w_down)).astype(jnp.bfloat16)
    saved = (live, normed_b, attended_b, mixed_b, normed2_b, act_b, pull_first, pull_core, pull_second, pull_act)
    return (layer_output, saved)

def backward_pass(cotangent, saved, mix_weights, ffn_weights, local_grads):
    w_query, key_value_weight, w_mixer_in, w_mixer_out, w_attn_out = mix_weights
    w_gate_up, w_down = ffn_weights
    live, normed_b, attended_b, mixed_b, normed2_b, act_b, pull_first, pull_core, pull_second, pull_act = saved
    wide_cot = cotangent.astype(jnp.float32)
    d_out = (live * wide_cot).astype(jnp.bfloat16)
    d_gate_up, = pull_act(product_nt(d_out, w_down))
    d_gate_up = d_gate_up.astype(jnp.bfloat16)
    d_middle_norm, grad_ffn_gain = pull_second(product_nt(d_gate_up, w_gate_up))
    d_middle = wide_cot + d_middle_norm
    d_branch = (live * d_middle).astype(jnp.bfloat16)
    d_core = pull_core((product_nt(d_branch, w_attn_out), product_nt(d_branch, w_mixer_out)))
    d_query = d_core[0].astype(jnp.bfloat16)
    d_keyval = d_core[1].astype(jnp.bfloat16)
    d_mixer_in = d_core[2].astype(jnp.bfloat16)
    d_normed = product_nt(d_query, w_query) + product_nt(d_keyval, key_value_weight) + product_nt(d_mixer_in, w_mixer_in)
    d_input_norm, grad_norm_gain = pull_first(d_normed)
    grad_rows = d_middle + d_input_norm
    lefts = (normed_b, mixed_b, attended_b, normed2_b, act_b)
    rights = (d_query, d_keyval, d_mixer_in, d_branch, d_gate_up, d_out)
    big = None
    if local_grads:
        big = (product_tn(normed_b, d_query), product_tn(normed_b, d_keyval), product_tn(normed_b, d_mixer_in), product_tn(mixed_b, d_branch), product_tn(attended_b, d_branch), product_tn(normed2_b, d_gate_up), product_tn(act_b, d_out))
    small = (grad_norm_gain, d_core[3], d_core[4], d_core[5], d_core[6], d_core[7], d_core[8], grad_ffn_gain)
    return (grad_rows, big, small, lefts, rights)

def reference(layer_input, segment_ids, cotangent, norm_gain, w_query, key_value_weight, w_mixer_in, conv_weight, conv_bias, dt_bias, decay_log, skip_gain, mixer_gain, w_mixer_out, w_attn_out, ffn_gain, w_gate_up, w_down):
    tile_count = TOKENS // TOK_DEV
    per_step = math.gcd(tile_count, max(1, 4096 // TOK_DEV))
    mix_weights = (w_query, key_value_weight, w_mixer_in, w_mixer_out, w_attn_out)
    ffn_weights = (w_gate_up, w_down)
    params = (norm_gain, conv_weight, conv_bias, dt_bias, decay_log, skip_gain, mixer_gain, ffn_gain)

    def one_tile(rows, segments, cot_rows):
        layer_rows, saved = forward_pass(rows, segments, mix_weights, ffn_weights, params)
        grad_rows, big, small, lefts, rights = backward_pass(cot_rows, saved, mix_weights, ffn_weights, True)
        return (layer_rows, grad_rows, big, small)

    def advance(carry, block):
        rows, segments, cot_rows = block
        layer_rows, grad_rows, big, small = jax.vmap(one_tile)(rows, segments, cot_rows)
        carry = jax.tree.map(lambda total, update: total + lax.optimization_barrier(jnp.sum(update, axis=0)), carry, (big, small))
        return (carry, (layer_rows, grad_rows))
    steps_total = tile_count // per_step
    blocks = (layer_input.reshape(steps_total, per_step, TOK_DEV, MODEL_WIDTH), segment_ids.reshape(steps_total, per_step, TOK_DEV), cotangent.reshape(steps_total, per_step, TOK_DEV, MODEL_WIDTH))
    start = jax.tree.map(lambda weight: jnp.zeros(weight.shape, jnp.float32), (mix_weights + ffn_weights, params))
    (big, small), (layer_rows, grad_rows) = lax.scan(advance, start, blocks)
    layer_output = layer_rows.reshape(TOKENS, MODEL_WIDTH)
    grad_input = grad_rows.reshape(TOKENS, MODEL_WIDTH)
    return (layer_output, grad_input, small[0], big[0], big[1], big[2], small[1], small[2], small[3], small[4], small[5], small[6], big[3], big[4], small[7], big[5], big[6])
```

```python
import functools
import math

import jax
import jax.numpy as jnp
from jax import lax
from jax.sharding import PartitionSpec as P

FF = 2048
MH = 24
HEAD_SIZE = 64
NS = 128
KC = 4
QUERY_HEADS = 8
KEY_VALUE_HEADS = 2
DI = 1536
CONV = 1792


EPS = 1e-05
ROPE_BASE = 100000000000.0


def product(left, right):
    return jnp.dot(left, right, preferred_element_type=jnp.float32)


def product_tn(left, right):
    return lax.dot_general(
        left, right, (((0,), (0,)), ((), ())), preferred_element_type=jnp.float32
    )


def product_nt(left, right):
    return lax.dot_general(
        left, right, (((1,), (1,)), ((), ())), preferred_element_type=jnp.float32
    )


def rms_norm(values, gain):
    return values * lax.rsqrt(jnp.mean(values * values, axis=-1, keepdims=True) + EPS) * gain


def positions_of(segments):
    item_count = segments.shape[0]
    index = jnp.arange(item_count, dtype=jnp.int32)
    starts = jnp.concatenate([jnp.ones((1,), bool), segments[1:] != segments[:-1]])
    begin = lax.cummax(jnp.where(starts, index, 0), axis=0)
    return index - begin


def rotate(values, position):
    half = HEAD_SIZE // 2
    freqs = ROPE_BASE ** (-2.0 * jnp.arange(half, dtype=jnp.float32) / HEAD_SIZE)
    angles = position.astype(jnp.float32)[:, None] * freqs[None, :]
    cosine = jnp.cos(angles)[:, None, :]
    sine = jnp.sin(angles)[:, None, :]
    first = values[..., :half]
    second = values[..., half:]
    return jnp.concatenate(
        [first * cosine - second * sine, second * cosine + first * sine], axis=-1
    )


def silu(values):
    return values / (1.0 + jnp.exp(-values))


def mixer_core(
    query,
    key_value,
    mixer_in,
    conv_weight,
    conv_bias,
    dt_bias,
    decay_log,
    skip_gain,
    mixer_gain,
    position,
    allowed,
    same_seg,
):
    item_count = query.shape[0]
    heads_q = query.reshape(item_count, QUERY_HEADS, HEAD_SIZE)
    paired_items = key_value.reshape(item_count, 2, KEY_VALUE_HEADS, HEAD_SIZE)
    keys = rotate(paired_items[:, 0], position)
    values = paired_items[:, 1]
    heads_q = rotate(heads_q, position)
    shard_group = QUERY_HEADS // KEY_VALUE_HEADS
    keys = jnp.repeat(keys, shard_group, axis=1)
    values = jnp.repeat(values, shard_group, axis=1)
    scores = jnp.einsum("thd,shd->hts", heads_q, keys, precision=lax.Precision.HIGHEST) / math.sqrt(
        HEAD_SIZE
    )
    scores = jnp.where(allowed[None], scores, -jnp.inf)
    highest = jnp.max(scores, axis=-1, keepdims=True)
    expo = jnp.exp(scores - highest)
    probs = expo / jnp.sum(expo, axis=-1, keepdims=True)
    attended = jnp.einsum("hts,shd->thd", probs, values, precision=lax.Precision.HIGHEST).reshape(
        item_count, QUERY_HEADS * HEAD_SIZE
    )
    gate_z = mixer_in[:, :DI]
    conv_in = mixer_in[:, DI : DI + CONV]
    dt_raw = mixer_in[:, DI + CONV :]
    total = jnp.zeros((item_count, CONV), jnp.float32) + conv_bias[None, :]
    for offset in range(KC):
        shifted = jnp.concatenate(
            [jnp.zeros((offset, CONV), jnp.float32), conv_in[: item_count - offset]], axis=0
        )
        total = total + conv_weight[KC - 1 - offset][None, :] * shifted * same_seg[offset][:, None]
    conv_out = silu(total)
    inner = conv_out[:, :DI].reshape(item_count, MH, HEAD_SIZE)
    bmat = conv_out[:, DI : DI + NS]
    cmat = conv_out[:, DI + NS :]
    step = jax.nn.softplus(dt_raw + dt_bias[None, :])
    csum = jnp.cumsum(step * (-jnp.exp(decay_log))[None, :], axis=0)
    gaps = csum[:, None, :] - csum[None, :, :]
    decay = jnp.exp(jnp.where(allowed[:, :, None], gaps, -jnp.inf))
    gram = jnp.dot(cmat, bmat.T, precision=lax.Precision.HIGHEST)
    mixing = gram[:, :, None] * decay * step[None, :, :]
    outputs = jnp.einsum("tsh,shp->thp", mixing, inner, precision=lax.Precision.HIGHEST)
    outputs = outputs + skip_gain[None, :, None] * inner
    gated = outputs.reshape(item_count, DI) * silu(gate_z)
    return (attended, rms_norm(gated, mixer_gain))


def swiglu(gate_up):
    return silu(gate_up[:, :FF]) * gate_up[:, FF:]


LANES = 128


def bit_count(size):
    return size.bit_length() - 1


def orders_of(size):
    bits = list(range(bit_count(size)))
    outer = bits[1:]
    return (outer + bits[:1], outer[::-1] + bits[:1])


def place_of(member, order):
    place = 0
    for position, bit in enumerate(order):
        place = place + (((member >> bit) & 1) << position)
    return place


def swap(values, axis_name, size, flip):
    return lax.ppermute(values, axis_name, [(i, i ^ flip) for i in range(size)])


def shift(values, axis_name, size, by):
    return lax.ppermute(values, axis_name, [(i, (i + by) % size) for i in range(size)])


def joined(values, other, bit, axis):
    low = ((lax.axis_index("rep") >> bit) & 1) == 0
    return jnp.concatenate([jnp.where(low, values, other), jnp.where(low, other, values)], axis=axis)


def gather_columns(piece, size, order):
    for bit in order:
        piece = joined(piece, swap(piece, "rep", size, 1 << bit), bit, 1)
    return piece


def gather_rows(piece, size, order, place_order):
    count = bit_count(size)
    rows, width = piece.shape
    piece = piece.reshape((1,) * count + (rows, width))
    for bit in order:
        axis = count - 1 - place_order.index(bit)
        piece = joined(piece, swap(piece, "rep", size, 1 << bit), bit, axis)
    return piece.reshape(size * rows, width)


def gather_tokens(rows, size, order):
    for bit in order:
        rows = jnp.concatenate([rows, swap(rows, "rep", size, 1 << bit)], axis=0)
    return rows


def exchange_columns(rows, size, order, token_order):
    member = lax.axis_index("rep")
    width = rows.shape[1] // size
    offsets = [0]
    for bit in token_order:
        offsets = offsets + [offset ^ (1 << bit) for offset in offsets]
    parts = []
    for offset in offsets:
        target = place_of(member ^ offset, order)
        part = lax.dynamic_slice_in_dim(rows, target * width, width, axis=1)
        parts.append(part if offset == 0 else swap(part, "rep", size, offset))
    return jnp.concatenate(parts, axis=0)


def gather_weight(shard, size, shards, orders):
    rows = shard.shape[0] // size
    place = place_of(lax.axis_index("rep"), orders[0])
    moving = lax.dynamic_slice_in_dim(shard, place * rows, rows, axis=0)
    found = [shard]
    for step in range(1, shards):
        moving = shift(moving, "shard", shards, 1)
        found.append(gather_rows(moving, size, orders[step % len(orders)], orders[0]))
    return found


def rows_of_step(values, step, shards):
    width = values.shape[1] // shards
    owner = (lax.axis_index("shard") + (shards - step)) % shards
    return lax.dynamic_slice_in_dim(values, owner * width, width, axis=1)


def times(left, weight):
    shards = len(weight)
    total = product(rows_of_step(left, 0, shards), weight[0])
    for step in range(1, shards):
        total = total + product(rows_of_step(left, step, shards), weight[step])
    return total


def times_transposed(left, weight):
    shards = len(weight)
    parts = [product_nt(left, part) for part in weight[::-1]]
    width = parts[0].shape[1]
    twice = jnp.concatenate(parts + parts[:-1], axis=1)
    start = (shards - 1 - lax.axis_index("shard")) * width
    return lax.dynamic_slice_in_dim(twice, start, shards * width, axis=1)


def weight_gradient(lefts, rights, size, shards, order):
    total = product_tn(rows_of_step(lefts, 0, shards), rights)
    for step in range(1, shards):
        part = product_tn(rows_of_step(lefts, shards - step, shards), rights)
        total = total + shift(part.astype(jnp.bfloat16), "shard", shards, step).astype(jnp.float32)
    return gather_columns(total.astype(jnp.bfloat16), size, order)


def total_of(values, size, shards):
    for bit in range(bit_count(size)):
        values = values + swap(values, "rep", size, 1 << bit)
    for bit in range(bit_count(shards)):
        values = values + swap(values, "shard", shards, 1 << bit)
    return values


def grouped(first, second, shards):
    item_count = first.shape[0]
    return jnp.concatenate(
        [first.reshape(item_count, shards, -1), second.reshape(item_count, shards, -1)], axis=2
    ).reshape(item_count, -1)


def ungrouped(values, first, shards):
    item_count = values.shape[0]
    values = values.reshape(item_count, shards, -1)
    return (
        values[:, :, : first // shards].reshape(item_count, -1),
        values[:, :, first // shards :].reshape(item_count, -1),
    )


def layer(
    size,
    shards,
    rows,
    segments,
    cotangent,
    norm_gain,
    w_query,
    key_value_weight,
    w_mixer_in,
    conv_weight,
    conv_bias,
    dt_bias,
    decay_log,
    skip_gain,
    mixer_gain,
    w_mixer_out,
    w_attn_out,
    ffn_gain,
    w_gate_up,
    w_down,
):
    first, second = orders_of(size)
    one, two = (first, second), (second, first)
    w_in = gather_weight(
        jnp.concatenate([w_query, key_value_weight, w_mixer_in], axis=1), size, shards, one
    )
    w_out = gather_weight(jnp.concatenate([w_attn_out, w_mixer_out], axis=0), size, shards, two)
    w_gate_up = gather_weight(w_gate_up, size, shards, two)
    w_down = gather_weight(w_down, size, shards, one)
    query_width, pair_width = w_query.shape[1], key_value_weight.shape[1]
    attended_width = w_attn_out.shape[0] * shards
    in_width = query_width + pair_width + w_mixer_in.shape[1]

    item_count = rows.shape[0]
    index = jnp.arange(item_count, dtype=jnp.int32)
    live = (segments >= 0).astype(jnp.float32)[:, None]
    allowed = (segments[:, None] == segments[None, :]) & (index[:, None] >= index[None, :])
    position = positions_of(segments)
    same_seg = jnp.stack(
        [
            jnp.concatenate(
                [
                    jnp.zeros((offset,), jnp.float32),
                    (segments[offset:] == segments[: item_count - offset]).astype(jnp.float32),
                ]
            )
            for offset in range(KC)
        ]
    )
    wide = rows.astype(jnp.float32)
    wide_cot = cotangent.astype(jnp.float32)
    d_out = (live * wide_cot).astype(jnp.bfloat16)
    normed, pull_first = jax.vjp(rms_norm, wide, norm_gain)
    normed_b = normed.astype(jnp.bfloat16)
    projected = times(normed_b, w_in)
    query = projected[:, :query_width]
    key_value = projected[:, query_width : query_width + pair_width]
    mixer_in = projected[:, query_width + pair_width :]

    def core(*values):
        return mixer_core(*values, position, allowed, same_seg)

    (attended, mixed), pull_core = jax.vjp(
        core,
        query,
        key_value,
        mixer_in,
        conv_weight,
        conv_bias,
        dt_bias,
        decay_log,
        skip_gain,
        mixer_gain,
    )
    branches = grouped(attended.astype(jnp.bfloat16), mixed.astype(jnp.bfloat16), shards)
    middle = wide + live * times(branches, w_out)
    normed2, pull_second = jax.vjp(rms_norm, middle, ffn_gain)
    normed2_b = normed2.astype(jnp.bfloat16)
    gate_up = times(normed2_b, w_gate_up)
    act, pull_act = jax.vjp(swiglu, gate_up)
    act_b = act.astype(jnp.bfloat16)
    layer_output = (middle + live * times(act_b, w_down)).astype(jnp.bfloat16)

    (d_gate_up,) = pull_act(times_transposed(d_out, w_down))
    d_gate_up = d_gate_up.astype(jnp.bfloat16)
    d_middle_norm, grad_ffn_gain = pull_second(times_transposed(d_gate_up, w_gate_up))
    d_middle = wide_cot + d_middle_norm
    d_branch = (live * d_middle).astype(jnp.bfloat16)
    d_core = pull_core(ungrouped(times_transposed(d_branch, w_out), attended_width, shards))
    d_in = jnp.concatenate([part.astype(jnp.bfloat16) for part in d_core[:3]], axis=1)
    d_input_norm, grad_norm_gain = pull_first(times_transposed(d_in, w_in))
    grad_input = d_middle + d_input_norm

    unit = size * LANES
    padded = jnp.pad(d_in, ((0, 0), (0, -in_width % unit)))

    def gradient(left, right, order, token_order):
        return weight_gradient(
            gather_tokens(left, size, token_order),
            exchange_columns(right, size, order, token_order),
            size,
            shards,
            order,
        ).astype(jnp.float32)

    grad_down = gradient(act_b, d_out, first, second)
    grad_gate_up = gradient(normed2_b, d_gate_up, second, first)
    grad_out = gradient(branches, d_branch, first, second)
    grad_in = gradient(normed_b, padded, second, first)
    small = (grad_norm_gain, *d_core[3:], grad_ffn_gain)
    flat = jnp.concatenate([part.reshape(-1) for part in small])
    flat = jnp.pad(flat, (0, -flat.shape[0] % (8 * LANES))).reshape(-1, LANES)
    flat = total_of(flat, size, shards).reshape(-1)
    summed = []
    start = 0
    for part in small:
        summed.append(flat[start : start + part.size].reshape(part.shape))
        start += part.size
    pair_end = query_width + pair_width
    return (
        layer_output,
        grad_input,
        summed[0],
        grad_in[:, :query_width],
        grad_in[:, query_width:pair_end],
        grad_in[:, pair_end:in_width],
        *summed[1:7],
        grad_out[attended_width // shards :],
        grad_out[: attended_width // shards],
        summed[7],
        grad_gate_up,
        grad_down,
    )


def solution(mesh):
    return jax.shard_map(
        functools.partial(layer, mesh.shape["rep"], mesh.shape["shard"]),
        mesh=mesh,
        in_specs=(
            P(("rep", "shard"), None),
            P(("rep", "shard")),
            P(("rep", "shard"), None),
            P(),
            P("shard", None),
            P("shard", None),
            P("shard", None),
            P(),
            P(),
            P(),
            P(),
            P(),
            P(),
            P("shard", None),
            P("shard", None),
            P(),
            P("shard", None),
            P("shard", None),
        ),
        out_specs=(
            P(("rep", "shard"), None),
            P(("rep", "shard"), None),
            P(),
            P("shard", None),
            P("shard", None),
            P("shard", None),
            P(),
            P(),
            P(),
            P(),
            P(),
            P(),
            P("shard", None),
            P("shard", None),
            P(),
            P("shard", None),
            P("shard", None),
        ),
        check_vma=False,
    )
```

```python
import functools
import math

import jax
import jax.numpy as jnp
from jax import lax
from jax.experimental import pallas as pl
from jax.experimental.pallas import tpu as pltpu
from jax.sharding import PartitionSpec as P

FF = 2048
MH = 24
HEAD_SIZE = 64
NS = 128
KC = 4
QUERY_HEADS = 8
KEY_VALUE_HEADS = 2
DI = 1536
CONV = 1792


EPS = 1e-05
ROPE_BASE = 100000000000.0


def product(left, right):
    return jnp.dot(left, right, preferred_element_type=jnp.float32)


def product_tn(left, right):
    return lax.dot_general(
        left, right, (((0,), (0,)), ((), ())), preferred_element_type=jnp.float32
    )


def product_nt(left, right):
    return lax.dot_general(
        left, right, (((1,), (1,)), ((), ())), preferred_element_type=jnp.float32
    )


def rms_norm(values, gain):
    return values * lax.rsqrt(jnp.mean(values * values, axis=-1, keepdims=True) + EPS) * gain


def positions_of(segments):
    item_count = segments.shape[0]
    index = jnp.arange(item_count, dtype=jnp.int32)
    starts = jnp.concatenate([jnp.ones((1,), bool), segments[1:] != segments[:-1]])
    begin = lax.cummax(jnp.where(starts, index, 0), axis=0)
    return index - begin


def rotate(values, position):
    half = HEAD_SIZE // 2
    freqs = ROPE_BASE ** (-2.0 * jnp.arange(half, dtype=jnp.float32) / HEAD_SIZE)
    angles = position.astype(jnp.float32)[:, None] * freqs[None, :]
    cosine = jnp.cos(angles)[:, None, :]
    sine = jnp.sin(angles)[:, None, :]
    first = values[..., :half]
    second = values[..., half:]
    return jnp.concatenate(
        [first * cosine - second * sine, second * cosine + first * sine], axis=-1
    )


def silu(values):
    return values / (1.0 + jnp.exp(-values))


def attention_core(query, key_value, position, allowed):
    item_count = query.shape[0]
    heads_q = query.reshape(item_count, QUERY_HEADS, HEAD_SIZE)
    paired_items = key_value.reshape(item_count, 2, KEY_VALUE_HEADS, HEAD_SIZE)
    keys = rotate(paired_items[:, 0], position)
    values = paired_items[:, 1]
    heads_q = rotate(heads_q, position)
    shard_group = QUERY_HEADS // KEY_VALUE_HEADS
    keys = jnp.repeat(keys, shard_group, axis=1)
    values = jnp.repeat(values, shard_group, axis=1)
    scores = jnp.einsum("thd,shd->hts", heads_q, keys, precision=lax.Precision.HIGHEST) / math.sqrt(
        HEAD_SIZE
    )
    scores = jnp.where(allowed[None], scores, -jnp.inf)
    highest = jnp.max(scores, axis=-1, keepdims=True)
    expo = jnp.exp(scores - highest)
    probs = expo / jnp.sum(expo, axis=-1, keepdims=True)
    return jnp.einsum("hts,shd->thd", probs, values, precision=lax.Precision.HIGHEST).reshape(
        item_count, QUERY_HEADS * HEAD_SIZE
    )


def mixer_core(
    mixer_in,
    conv_weight,
    conv_bias,
    dt_bias,
    decay_log,
    skip_gain,
    mixer_gain,
    allowed,
    same_seg,
):
    item_count = mixer_in.shape[0]
    gate_z = mixer_in[:, :DI]
    conv_in = mixer_in[:, DI : DI + CONV]
    dt_raw = mixer_in[:, DI + CONV :]
    total = jnp.zeros((item_count, CONV), jnp.float32) + conv_bias[None, :]
    for offset in range(KC):
        shifted = jnp.concatenate(
            [jnp.zeros((offset, CONV), jnp.float32), conv_in[: item_count - offset]], axis=0
        )
        total = total + conv_weight[KC - 1 - offset][None, :] * shifted * same_seg[offset][:, None]
    conv_out = silu(total)
    inner = conv_out[:, :DI].reshape(item_count, MH, HEAD_SIZE)
    bmat = conv_out[:, DI : DI + NS]
    cmat = conv_out[:, DI + NS :]
    step = jax.nn.softplus(dt_raw + dt_bias[None, :])
    csum = jnp.cumsum(step * (-jnp.exp(decay_log))[None, :], axis=0)
    gaps = csum[:, None, :] - csum[None, :, :]
    decay = jnp.exp(jnp.where(allowed[:, :, None], gaps, -jnp.inf))
    gram = jnp.dot(cmat, bmat.T, precision=lax.Precision.HIGHEST)
    mixing = gram[:, :, None] * decay * step[None, :, :]
    outputs = jnp.einsum("tsh,shp->thp", mixing, inner, precision=lax.Precision.HIGHEST)
    outputs = outputs + skip_gain[None, :, None] * inner
    gated = outputs.reshape(item_count, DI) * silu(gate_z)
    return rms_norm(gated, mixer_gain)


def swiglu(gate_up):
    return silu(gate_up[:, :FF]) * gate_up[:, FF:]


LANES = 128
SUBLANES = 8


def bit_count(size):
    return size.bit_length() - 1


def swap(values, axis_name, size, flip):
    return lax.ppermute(values, axis_name, [(i, i ^ flip) for i in range(size)])


def shift(values, axis_name, size, by):
    return lax.ppermute(values, axis_name, [(i, (i + by) % size) for i in range(size)])


def together(*values):
    return lax.optimization_barrier(values)


def after(values, done):
    return lax.optimization_barrier((values, done))[0]


def spread_first(piece, size, order):
    stacked, offsets = piece[None], [0]
    for bit in order[:-1]:
        stacked = jnp.concatenate([stacked, swap(stacked, "rep", size, 1 << bit)], axis=0)
        offsets = offsets + [offset ^ (1 << bit) for offset in offsets]
    return stacked, offsets


def spread_second(stacked, offsets, size, order):
    groups = [(stacked, offsets)]
    if order:
        flip = 1 << order[-1]
        groups.append((swap(stacked, "rep", size, flip), [offset ^ flip for offset in offsets]))
    return groups


def spread_core(groups, size):
    return groups + [
        (swap(part, "rep", size, 1), [place ^ 1 for place in places]) for part, places in groups
    ]


def spread(piece, size, order):
    return spread_core(spread_second(*spread_first(piece, size, order), size, order), size)


def assemble(shard, halves, size, shards):
    rows, width = shard.shape
    piece = rows // size
    half = piece // len(halves)

    def copies(me, own):
        yield own * rows, None, None, None, None
        for which, groups in enumerate(halves):
            for part, (_, places) in enumerate(groups):
                for slot, place in enumerate(places):
                    for step in range(1, shards):
                        owner = (own + (shards - step)) % shards
                        start = owner * rows + (me ^ place) * piece + which * half
                        yield start, which, part, slot, step - 1

    flat = [part for groups in halves for part, _ in groups]
    per_half = len(halves[0])
    if half % SUBLANES != 0:
        own = lax.axis_index("shard")
        whole = jnp.zeros((rows * shards, width), shard.dtype)
        for start, which, part, slot, step in copies(lax.axis_index("rep"), own):
            block = shard if which is None else flat[which * per_half + part][slot, step]
            whole = lax.dynamic_update_slice_in_dim(whole, block, start, axis=0)
        return whole

    def kernel(own_ref, *refs):
        *parts, whole_ref, sem = refs
        started = []
        me, own = lax.axis_index("rep"), lax.axis_index("shard")
        for number, (start, which, part, slot, step) in enumerate(copies(me, own)):
            start = pl.multiple_of(start, SUBLANES)
            if which is None:
                source, size_rows = own_ref, rows
            else:
                source, size_rows = parts[which * per_half + part].at[slot, step], half
            copy = pltpu.make_async_copy(source, whole_ref.at[pl.ds(start, size_rows)], sem.at[number])
            copy.start()
            started.append(copy)
        for copy in started:
            copy.wait()

    total = 1 + sum(len(places) * (shards - 1) for groups in halves for _, places in groups)
    return pl.pallas_call(
        kernel,
        out_shape=jax.ShapeDtypeStruct((rows * shards, width), shard.dtype),
        in_specs=[pl.BlockSpec(memory_space=pl.ANY)] * (1 + len(flat)),
        out_specs=pl.BlockSpec(memory_space=pl.ANY),
        scratch_shapes=[pltpu.SemaphoreType.DMA((total,))],
    )(shard, *flat)


def ring_pieces(piece, shards):
    found = []
    for _ in range(1, shards):
        piece = shift(piece, "shard", shards, 1)
        found.append(piece)
    return jnp.stack(found)


def own_piece(shard, size):
    rows = shard.shape[0] // size
    return lax.dynamic_slice_in_dim(shard, lax.axis_index("rep") * rows, rows, axis=0)


def double_tokens(rows, size, bit):
    return jnp.concatenate([rows, swap(rows, "rep", size, 1 << bit)], axis=0)


def pair_tokens(rows, size):
    return jnp.stack([rows, swap(rows, "rep", size, 1)])


def halve_columns(rows, size, bit):
    half = rows.shape[2] // 2
    mine = ((lax.axis_index("rep") >> bit) & 1) * half
    kept = lax.dynamic_slice_in_dim(rows, mine, half, axis=2)
    sent = lax.dynamic_slice_in_dim(rows, half - mine, half, axis=2)
    return jnp.concatenate([kept, swap(sent, "rep", size, 1 << bit)], axis=0 if bit == 0 else 1)


def column_place(member, order):
    place = 0
    for bit in [0] + order:
        place = place * 2 + ((member >> bit) & 1)
    return place


def column_gradient(lefts, rights):
    return lax.dot_general(
        lefts, rights, (((0, 1), (0, 1)), ((), ())), preferred_element_type=jnp.float32
    ).astype(jnp.bfloat16)


def scatter_shards(parts, shards):
    own = lax.axis_index("shard")

    def part_of(place):
        return lax.dynamic_index_in_dim(parts, place, axis=0, keepdims=False)

    total = part_of(own).astype(jnp.float32)
    for step in range(1, shards):
        part = part_of((own + step) % shards)
        total = total + shift(part, "shard", shards, step).astype(jnp.float32)
    return total.astype(jnp.bfloat16)


def gather_columns(piece, size, order, write, out_shapes):
    groups = spread(piece, size, order[::-1])
    blocks = jnp.concatenate([part for part, _ in groups], axis=0)

    def kernel(blocks_ref, *outs):
        mine = column_place(lax.axis_index("rep"), order)
        for place in range(size):
            write(place, blocks_ref[mine ^ place].astype(jnp.float32), outs)

    return pl.pallas_call(
        kernel,
        out_shape=[jax.ShapeDtypeStruct(shape, jnp.float32) for shape in out_shapes],
        in_specs=[pl.BlockSpec(memory_space=pltpu.VMEM)],
        out_specs=[pl.BlockSpec(memory_space=pltpu.VMEM)] * len(out_shapes),
    )(blocks)


def total_of(values, size, shards):
    for bit in range(bit_count(size)):
        values = values + swap(values, "rep", size, 1 << bit)
    for bit in range(bit_count(shards)):
        values = values + swap(values, "shard", shards, 1 << bit)
    return values


def grouped(first, second, shards):
    item_count = first.shape[0]
    return jnp.concatenate(
        [first.reshape(item_count, shards, -1), second.reshape(item_count, shards, -1)], axis=2
    ).reshape(item_count, -1)


def ungrouped(values, first, shards):
    item_count = values.shape[0]
    values = values.reshape(item_count, shards, -1)
    return (
        values[:, :, : first // shards].reshape(item_count, -1),
        values[:, :, first // shards :].reshape(item_count, -1),
    )


def blocked(arrays, size, backwards=False):
    item_count = arrays[0].shape[0]
    count = bit_count(size)
    values = jnp.concatenate(
        [values.reshape(item_count, size, -1) for values in arrays], axis=2
    )
    if backwards:
        values = values.reshape((item_count,) + (2,) * count + (-1,))
        axes = [0, 1] + list(range(count, 1, -1)) + [count + 1]
        values = values.transpose(axes)
    return values.reshape(1, item_count, -1)


def layer(
    size,
    shards,
    rows,
    segments,
    cotangent,
    norm_gain,
    w_query,
    key_value_weight,
    w_mixer_in,
    conv_weight,
    conv_bias,
    dt_bias,
    decay_log,
    skip_gain,
    mixer_gain,
    w_mixer_out,
    w_attn_out,
    ffn_gain,
    w_gate_up,
    w_down,
):
    one = list(range(1, bit_count(size)))
    two = one[::-1]
    in_shard = jnp.concatenate([w_query, key_value_weight, w_mixer_in], axis=1)
    out_shard = jnp.concatenate([w_attn_out, w_mixer_out], axis=0)
    half_in = in_shard.shape[0] // size // 2
    half_gate_up = w_gate_up.shape[0] // size // 2
    out_piece_rows = out_shard.shape[0] // size
    in_pieces = ring_pieces(own_piece(in_shard, size), shards)
    out_piece, gate_up_piece = after(
        (
            jnp.concatenate([own_piece(out_shard, size), own_piece(w_down, size)], axis=0),
            own_piece(w_gate_up, size),
        ),
        in_pieces,
    )
    out_pieces = ring_pieces(out_piece, shards)
    gate_up_pieces = ring_pieces(gate_up_piece, shards)
    in_first = [
        spread_first(in_pieces[:, :half_in], size, one),
        spread_first(in_pieces[:, half_in:], size, two),
    ]
    in_second = [
        spread_second(*in_first[0], size, one),
        spread_second(*in_first[1], size, two),
    ]
    out_pieces, gate_up_pieces = after(
        (out_pieces, gate_up_pieces), [[part for part, _ in groups] for groups in in_second]
    )
    w_in = assemble(in_shard, [spread_core(groups, size) for groups in in_second], size, shards)
    rest_orders = (one, two, one, two)
    rest_first = [
        spread_first(piece, size, order)
        for piece, order in zip(
            (
                out_pieces[:, :out_piece_rows],
                out_pieces[:, out_piece_rows:],
                gate_up_pieces[:, :half_gate_up],
                gate_up_pieces[:, half_gate_up:],
            ),
            rest_orders,
        )
    ]
    query_width, pair_width = w_query.shape[1], key_value_weight.shape[1]
    attended_width = w_attn_out.shape[0] * shards
    in_width = query_width + pair_width + w_mixer_in.shape[1]

    item_count = rows.shape[0]
    index = jnp.arange(item_count, dtype=jnp.int32)
    live = (segments >= 0).astype(jnp.float32)[:, None]
    allowed = (segments[:, None] == segments[None, :]) & (index[:, None] >= index[None, :])
    position = positions_of(segments)
    same_seg = jnp.stack(
        [
            jnp.concatenate(
                [
                    jnp.zeros((offset,), jnp.float32),
                    (segments[offset:] == segments[: item_count - offset]).astype(jnp.float32),
                ]
            )
            for offset in range(KC)
        ]
    )
    wide = rows.astype(jnp.float32)
    wide_cot = cotangent.astype(jnp.float32)
    d_out = (live * wide_cot).astype(jnp.bfloat16)
    normed, pull_first = jax.vjp(rms_norm, wide, norm_gain)
    normed_b = normed.astype(jnp.bfloat16)
    projected = product(normed_b, w_in)
    query = projected[:, :query_width]
    key_value = projected[:, query_width : query_width + pair_width]
    mixer_in = projected[:, query_width + pair_width :]

    attended, pull_attention = jax.vjp(
        lambda *values: attention_core(*values, position, allowed), query, key_value
    )
    stacks, mixer_in = together([stacked for stacked, _ in rest_first], mixer_in)
    rest_second = [
        spread_second(stacked, offsets, size, order)
        for stacked, (_, offsets), order in zip(stacks, rest_first, rest_orders)
    ]
    mixed, pull_mixer = jax.vjp(
        lambda *values: mixer_core(*values, allowed, same_seg),
        mixer_in,
        conv_weight,
        conv_bias,
        dt_bias,
        decay_log,
        skip_gain,
        mixer_gain,
    )
    arrived = [[part for part, _ in groups] for groups in rest_second]
    arrived, attended, mixed = together(arrived, attended, mixed)
    rest = [
        spread_core([(part, places) for part, (_, places) in zip(parts, groups)], size)
        for parts, groups in zip(arrived, rest_second)
    ]
    w_out = assemble(out_shard, rest[:1], size, shards)
    w_down = assemble(w_down, rest[1:2], size, shards)
    w_gate_up = assemble(w_gate_up, rest[2:], size, shards)
    branches = grouped(attended.astype(jnp.bfloat16), mixed.astype(jnp.bfloat16), shards)
    middle = wide + live * product(branches, w_out)
    normed2, pull_second = jax.vjp(rms_norm, middle, ffn_gain)
    normed2_b = normed2.astype(jnp.bfloat16)
    gate_up = product(normed2_b, w_gate_up)
    act, pull_act = jax.vjp(swiglu, gate_up)
    act_b = act.astype(jnp.bfloat16)
    early = double_tokens(jnp.concatenate([normed_b, branches], axis=1), size, one[0])
    late = double_tokens(jnp.concatenate([normed2_b, act_b], axis=1), size, two[0])
    layer_output = (middle + live * product(act_b, w_down)).astype(jnp.bfloat16)

    (d_gate_up,) = pull_act(product_nt(d_out, w_down))
    d_gate_up = d_gate_up.astype(jnp.bfloat16)
    late_rights = halve_columns(blocked([d_gate_up, d_out], size, True), size, 0)
    d_middle_norm, grad_ffn_gain = pull_second(product_nt(d_gate_up, w_gate_up))
    d_middle = wide_cot + d_middle_norm
    d_branch = (live * d_middle).astype(jnp.bfloat16)
    out_rights = halve_columns(blocked([d_branch], size), size, 0)
    d_attended, d_mixed = ungrouped(product_nt(d_branch, w_out), attended_width, shards)
    early, late, late_rights, out_rights, d_attended, d_mixed = together(
        early, late, late_rights, out_rights, d_attended, d_mixed
    )
    for bit in one[1:]:
        early = double_tokens(early, size, bit)
    for bit in two[1:]:
        late = double_tokens(late, size, bit)
    late_rights = halve_columns(late_rights, size, two[0])
    out_rights = halve_columns(out_rights, size, one[0])
    d_query, d_keyval = pull_attention(d_attended)
    late_rights, out_rights, d_mixed = together(late_rights, out_rights, d_mixed)
    for bit in two[1:]:
        late_rights = halve_columns(late_rights, size, bit)
    for bit in one[1:]:
        out_rights = halve_columns(out_rights, size, bit)
    d_mixer_in, *d_small = pull_mixer(d_mixed)
    early, late, late_rights, out_rights, d_mixer_in = together(
        early, late, late_rights, out_rights, d_mixer_in
    )
    d_in = jnp.concatenate(
        [part.astype(jnp.bfloat16) for part in (d_query, d_keyval, d_mixer_in)], axis=1
    )
    in_rights = halve_columns(
        jnp.pad(d_in, ((0, 0), (0, -in_width % (size * LANES))))[None], size, 0
    )
    early = pair_tokens(early, size)
    late = pair_tokens(late, size)
    for bit in one:
        in_rights = halve_columns(in_rights, size, bit)
    d_input_norm, grad_norm_gain = pull_first(product_nt(d_in, w_in))
    grad_input = d_middle + d_input_norm

    model, hidden = normed_b.shape[1], act_b.shape[1]
    gu_width, width = d_gate_up.shape[1] // size, model // size
    part_rows = model // shards

    def folded(gradient):
        values = gradient.reshape(shards, -1, part_rows, width)
        return [values[:, i] for i in range(values.shape[1])]

    parts = jnp.concatenate(
        [
            column_gradient(late[:, :, :model], late_rights[:, :, :gu_width]).reshape(
                shards, part_rows, gu_width
            ),
            *folded(column_gradient(late[:, :, model:], late_rights[:, :, gu_width:])),
            *folded(column_gradient(early[:, :, model:], out_rights)),
        ],
        axis=2,
    )
    attended_rows = attended_width // shards
    out_rows = branches.shape[1] // shards
    down_rows = hidden // shards

    def write_late(place, block, outs):
        gate_up_ref, down_ref, attended_ref, mixed_ref = outs
        gate_up_ref[:, place * gu_width : (place + 1) * gu_width] = block[:, :gu_width]
        columns = slice(place * width, (place + 1) * width)
        at = gu_width
        for row in range(0, down_rows, part_rows):
            down_ref[row : row + part_rows, columns] = block[:, at : at + width]
            at += width
        for row in range(0, out_rows, part_rows):
            values = block[:, at : at + width]
            at += width
            here = max(0, min(part_rows, attended_rows - row))
            if here:
                attended_ref[row : row + here, columns] = values[:here]
            if here < part_rows:
                start = row + here - attended_rows
                mixed_ref[start : start + part_rows - here, columns] = values[here:]

    grad_gate_up, grad_down, grad_attn_out, grad_mixer_out = gather_columns(
        scatter_shards(parts, shards),
        size,
        one,
        write_late,
        [
            (part_rows, d_gate_up.shape[1]),
            (down_rows, model),
            (attended_rows, model),
            (out_rows - attended_rows, model),
        ],
    )

    in_block = in_rights.shape[2]
    in_parts = column_gradient(early[:, :, :model], in_rights).reshape(
        shards, part_rows, in_block
    )

    def write_in(place, block, outs):
        start, stop = place * in_block, (place + 1) * in_block
        begin = 0
        for out_ref in outs:
            end = begin + out_ref.shape[1]
            low, high = max(start, begin), min(stop, end)
            if low < high:
                out_ref[:, low - begin : high - begin] = block[:, low - start : high - start]
            begin = end

    grad_query, grad_pair, grad_mixer_in = gather_columns(
        scatter_shards(in_parts, shards),
        size,
        one,
        write_in,
        [(part_rows, w.shape[1]) for w in (w_query, key_value_weight, w_mixer_in)],
    )
    small = (grad_norm_gain, *d_small, grad_ffn_gain)
    flat = jnp.concatenate([part.reshape(-1) for part in small])
    flat = jnp.pad(flat, (0, -flat.shape[0] % (8 * LANES))).reshape(-1, LANES)
    flat = total_of(flat, size, shards).reshape(-1)
    summed = []
    start = 0
    for part in small:
        summed.append(flat[start : start + part.size].reshape(part.shape))
        start += part.size
    return (
        layer_output,
        grad_input,
        summed[0],
        grad_query,
        grad_pair,
        grad_mixer_in,
        *summed[1:7],
        grad_mixer_out,
        grad_attn_out,
        summed[7],
        grad_gate_up,
        grad_down,
    )


def solution(mesh):
    return jax.shard_map(
        functools.partial(layer, mesh.shape["rep"], mesh.shape["shard"]),
        mesh=mesh,
        in_specs=(
            P(("rep", "shard"), None),
            P(("rep", "shard")),
            P(("rep", "shard"), None),
            P(),
            P("shard", None),
            P("shard", None),
            P("shard", None),
            P(),
            P(),
            P(),
            P(),
            P(),
            P(),
            P("shard", None),
            P("shard", None),
            P(),
            P("shard", None),
            P("shard", None),
        ),
        out_specs=(
            P(("rep", "shard"), None),
            P(("rep", "shard"), None),
            P(),
            P("shard", None),
            P("shard", None),
            P("shard", None),
            P(),
            P(),
            P(),
            P(),
            P(),
            P(),
            P("shard", None),
            P("shard", None),
            P(),
            P("shard", None),
            P("shard", None),
        ),
        check_vma=False,
    )
```

```python
import functools
import math

import jax
import jax.numpy as jnp
from jax import lax
from jax.experimental import pallas as pl
from jax.experimental.pallas import tpu as pltpu
from jax.sharding import PartitionSpec as P

FF = 2048
MH = 24
HEAD_SIZE = 64
NS = 128
KC = 4
QUERY_HEADS = 8
KEY_VALUE_HEADS = 2
DI = 1536
CONV = 1792


EPS = 1e-05
ROPE_BASE = 100000000000.0


def product(left, right):
    return jnp.dot(left, right, preferred_element_type=jnp.float32)


def product_tn(left, right):
    return lax.dot_general(
        left, right, (((0,), (0,)), ((), ())), preferred_element_type=jnp.float32
    )


def product_nt(left, right):
    return lax.dot_general(
        left, right, (((1,), (1,)), ((), ())), preferred_element_type=jnp.float32
    )


def rms_norm(values, gain):
    return values * lax.rsqrt(jnp.mean(values * values, axis=-1, keepdims=True) + EPS) * gain


def positions_of(segments):
    item_count = segments.shape[0]
    index = jnp.arange(item_count, dtype=jnp.int32)
    starts = jnp.concatenate([jnp.ones((1,), bool), segments[1:] != segments[:-1]])
    begin = lax.cummax(jnp.where(starts, index, 0), axis=0)
    return index - begin


def rotate(values, position):
    half = HEAD_SIZE // 2
    freqs = ROPE_BASE ** (-2.0 * jnp.arange(half, dtype=jnp.float32) / HEAD_SIZE)
    angles = position.astype(jnp.float32)[:, None] * freqs[None, :]
    cosine = jnp.cos(angles)[:, None, :]
    sine = jnp.sin(angles)[:, None, :]
    first = values[..., :half]
    second = values[..., half:]
    return jnp.concatenate(
        [first * cosine - second * sine, second * cosine + first * sine], axis=-1
    )


def silu(values):
    return values / (1.0 + jnp.exp(-values))


def attention_core(query, key_value, position, allowed):
    item_count = query.shape[0]
    heads_q = query.reshape(item_count, QUERY_HEADS, HEAD_SIZE)
    paired_items = key_value.reshape(item_count, 2, KEY_VALUE_HEADS, HEAD_SIZE)
    keys = rotate(paired_items[:, 0], position)
    values = paired_items[:, 1]
    heads_q = rotate(heads_q, position)
    shard_group = QUERY_HEADS // KEY_VALUE_HEADS
    keys = jnp.repeat(keys, shard_group, axis=1)
    values = jnp.repeat(values, shard_group, axis=1)
    scores = jnp.einsum("thd,shd->hts", heads_q, keys, precision=lax.Precision.HIGHEST) / math.sqrt(
        HEAD_SIZE
    )
    scores = jnp.where(allowed[None], scores, -jnp.inf)
    highest = jnp.max(scores, axis=-1, keepdims=True)
    expo = jnp.exp(scores - highest)
    probs = expo / jnp.sum(expo, axis=-1, keepdims=True)
    return jnp.einsum("hts,shd->thd", probs, values, precision=lax.Precision.HIGHEST).reshape(
        item_count, QUERY_HEADS * HEAD_SIZE
    )


def conv_core(conv_in, conv_weight, conv_bias, same_seg):
    item_count = conv_in.shape[0]
    total = jnp.zeros((item_count, CONV), jnp.float32) + conv_bias[None, :]
    for offset in range(KC):
        shifted = jnp.concatenate(
            [jnp.zeros((offset, CONV), jnp.float32), conv_in[: item_count - offset]], axis=0
        )
        total = total + conv_weight[KC - 1 - offset][None, :] * shifted * same_seg[offset][:, None]
    return silu(total)


def mixer_core(
    conv_out,
    gate_z,
    dt_raw,
    dt_bias,
    decay_log,
    skip_gain,
    mixer_gain,
    allowed,
):
    item_count = conv_out.shape[0]
    inner = conv_out[:, :DI].reshape(item_count, MH, HEAD_SIZE)
    bmat = conv_out[:, DI : DI + NS]
    cmat = conv_out[:, DI + NS :]
    step = jax.nn.softplus(dt_raw + dt_bias[None, :])
    csum = jnp.cumsum(step * (-jnp.exp(decay_log))[None, :], axis=0)
    gaps = csum[:, None, :] - csum[None, :, :]
    decay = jnp.exp(jnp.where(allowed[:, :, None], gaps, -jnp.inf))
    gram = jnp.dot(cmat, bmat.T, precision=lax.Precision.HIGHEST)
    mixing = gram[:, :, None] * decay * step[None, :, :]
    outputs = jnp.einsum("tsh,shp->thp", mixing, inner, precision=lax.Precision.HIGHEST)
    outputs = outputs + skip_gain[None, :, None] * inner
    gated = outputs.reshape(item_count, DI) * silu(gate_z)
    return rms_norm(gated, mixer_gain)


def swiglu(gate_up):
    return silu(gate_up[:, :FF]) * gate_up[:, FF:]


LANES = 128
SUBLANES = 8


def bit_count(size):
    return size.bit_length() - 1


def swap(values, axis_name, size, flip):
    return lax.ppermute(values, axis_name, [(i, i ^ flip) for i in range(size)])


def shift(values, axis_name, size, by):
    return lax.ppermute(values, axis_name, [(i, (i + by) % size) for i in range(size)])


def together(*values):
    return lax.optimization_barrier(values)


def after(values, done):
    return lax.optimization_barrier((values, done))[0]


def spread_first(piece, size, order):
    stacked, offsets = piece[None], [0]
    for bit in order[:-1]:
        stacked = jnp.concatenate([stacked, swap(stacked, "rep", size, 1 << bit)], axis=0)
        offsets = offsets + [offset ^ (1 << bit) for offset in offsets]
    return stacked, offsets


def spread_second(stacked, offsets, size, order):
    groups = [(stacked, offsets)]
    if order:
        flip = 1 << order[-1]
        groups.append((swap(stacked, "rep", size, flip), [offset ^ flip for offset in offsets]))
    return groups


def spread_core(groups, size):
    return groups + [
        (swap(part, "rep", size, 1), [place ^ 1 for place in places]) for part, places in groups
    ]


def spread(piece, size, order):
    return spread_core(spread_second(*spread_first(piece, size, order), size, order), size)


def assemble(shard, halves, size, shards):
    rows, width = shard.shape
    piece = rows // size
    half = piece // len(halves)

    def copies(me, own):
        yield own * rows, None, None, None, None
        for which, groups in enumerate(halves):
            for part, (_, places) in enumerate(groups):
                for slot, place in enumerate(places):
                    for step in range(1, shards):
                        owner = (own + (shards - step)) % shards
                        start = owner * rows + (me ^ place) * piece + which * half
                        yield start, which, part, slot, step - 1

    flat = [part for groups in halves for part, _ in groups]
    per_half = len(halves[0])
    if half % SUBLANES != 0:
        own = lax.axis_index("shard")
        whole = jnp.zeros((rows * shards, width), shard.dtype)
        for start, which, part, slot, step in copies(lax.axis_index("rep"), own):
            block = shard if which is None else flat[which * per_half + part][slot, step]
            whole = lax.dynamic_update_slice_in_dim(whole, block, start, axis=0)
        return whole

    def kernel(own_ref, *refs):
        *parts, whole_ref = refs
        me, own = lax.axis_index("rep"), lax.axis_index("shard")
        for start, which, part, slot, step in copies(me, own):
            start = pl.multiple_of(start, SUBLANES)
            if which is None:
                whole_ref[pl.ds(start, rows), :] = own_ref[...]
            else:
                whole_ref[pl.ds(start, half), :] = parts[which * per_half + part][slot, step]

    return pl.pallas_call(
        kernel,
        out_shape=jax.ShapeDtypeStruct((rows * shards, width), shard.dtype),
        in_specs=[pl.BlockSpec(memory_space=pltpu.VMEM)] * (1 + len(flat)),
        out_specs=pl.BlockSpec(memory_space=pltpu.VMEM),
    )(shard, *flat)


def ring_step(piece, shards):
    return shift(piece, "shard", shards, 1)


def own_piece(shard, size):
    rows = shard.shape[0] // size
    return lax.dynamic_slice_in_dim(shard, lax.axis_index("rep") * rows, rows, axis=0)


def outer_offsets(size):
    return [offset << 1 for offset in range(size // 2)]


def send_rows(rows, size):
    return [rows if offset == 0 else swap(rows, "rep", size, offset) for offset in outer_offsets(size)]


def pair_rows(parts, size):
    rows = jnp.concatenate(parts, axis=0)
    return rows, swap(rows, "rep", size, 1)


def halve_columns(rows, size):
    half = rows.shape[1] // 2
    mine = (lax.axis_index("rep") & 1) * half
    kept = lax.dynamic_slice_in_dim(rows, mine, half, axis=1)
    sent = lax.dynamic_slice_in_dim(rows, half - mine, half, axis=1)
    return jnp.stack([kept, swap(sent, "rep", size, 1)])


def send_columns(pair, size):
    width = pair.shape[2] // (size // 2)
    parts = []
    for offset in outer_offsets(size):
        target = (lax.axis_index("rep") ^ offset) >> 1
        part = lax.dynamic_slice_in_dim(pair, target * width, width, axis=2)
        parts.append(part if offset == 0 else swap(part, "rep", size, offset))
    return jnp.concatenate(parts, axis=1)


def column_gradient(lefts, rights, start, stop):
    return sum(
        product_tn(left[:, start:stop], right) for left, right in zip(lefts, (rights[0], rights[1]))
    ).astype(jnp.bfloat16)


def send_shards(parts, shards):
    own = lax.axis_index("shard")

    def part_of(place):
        return lax.dynamic_index_in_dim(parts, place, axis=0, keepdims=False)

    return [part_of(own)] + [
        shift(part_of((own + step) % shards), "shard", shards, step) for step in range(1, shards)
    ]


def sum_of(parts):
    return sum(part.astype(jnp.float32) for part in parts).astype(jnp.bfloat16)


def unpack_columns(own, near, size, write, out_shapes):
    half = size // 2

    def kernel(own_ref, near_ref, *outs):
        member = lax.axis_index("rep")
        for place in range(size):
            slot = (member >> 1) ^ (place % half)
            same = (member & 1) == place // half
            block = jnp.where(same, own_ref[slot].astype(jnp.float32), near_ref[slot].astype(jnp.float32))
            write(place, block, outs)

    return pl.pallas_call(
        kernel,
        out_shape=[jax.ShapeDtypeStruct(shape, jnp.float32) for shape in out_shapes],
        in_specs=[pl.BlockSpec(memory_space=pltpu.VMEM)] * 2,
        out_specs=[pl.BlockSpec(memory_space=pltpu.VMEM)] * len(out_shapes),
    )(own, near)


def total_of(values, size, shards):
    for bit in range(bit_count(size)):
        values = values + swap(values, "rep", size, 1 << bit)
    for bit in range(bit_count(shards)):
        values = values + swap(values, "shard", shards, 1 << bit)
    return values


def grouped(first, second, shards):
    one, two = first.shape[1] // shards, second.shape[1] // shards
    parts = []
    for i in range(shards):
        parts += [first[:, i * one : (i + 1) * one], second[:, i * two : (i + 1) * two]]
    return jnp.concatenate(parts, axis=1)


def ungrouped(values, first, shards):
    one, both = first // shards, values.shape[1] // shards
    starts = range(0, values.shape[1], both)
    return (
        jnp.concatenate([values[:, start : start + one] for start in starts], axis=1),
        jnp.concatenate([values[:, start + one : start + both] for start in starts], axis=1),
    )


def layer(
    size,
    shards,
    rows,
    segments,
    cotangent,
    norm_gain,
    w_query,
    key_value_weight,
    w_mixer_in,
    conv_weight,
    conv_bias,
    dt_bias,
    decay_log,
    skip_gain,
    mixer_gain,
    w_mixer_out,
    w_attn_out,
    ffn_gain,
    w_gate_up,
    w_down,
):
    one = list(range(1, bit_count(size)))
    two = one[::-1]
    in_shard = jnp.concatenate([w_query, key_value_weight, w_mixer_in], axis=1)
    out_shard = jnp.concatenate([w_attn_out, w_mixer_out], axis=0)
    half_in = in_shard.shape[0] // size // 2
    half_gate_up = w_gate_up.shape[0] // size // 2
    out_piece_rows = out_shard.shape[0] // size
    in_piece = jnp.concatenate(
        [own_piece(w, size) for w in (w_query, key_value_weight, w_mixer_in)], axis=1
    )
    in_pieces = []
    for _ in range(1, shards):
        in_piece = ring_step(in_piece, shards)
        in_pieces.append(in_piece)
    out_piece, gate_up_piece = after(
        (
            jnp.concatenate([own_piece(out_shard, size), own_piece(w_down, size)], axis=0),
            own_piece(w_gate_up, size),
        ),
        in_pieces,
    )
    in_pieces = jnp.stack(in_pieces)
    in_first = [
        spread_first(in_pieces[:, :half_in], size, one),
        spread_first(in_pieces[:, half_in:], size, two),
    ]
    in_second = [
        spread_second(*in_first[0], size, one),
        spread_second(*in_first[1], size, two),
    ]
    in_arrays = [[part for part, _ in groups] for groups in in_second]
    out_pieces, gate_up_pieces = [], []
    for step in range(1, shards):
        if step == shards - 1:
            out_piece, gate_up_piece = after((out_piece, gate_up_piece), in_arrays)
        out_piece = ring_step(out_piece, shards)
        gate_up_piece = ring_step(gate_up_piece, shards)
        out_pieces.append(out_piece)
        gate_up_pieces.append(gate_up_piece)
    w_in = assemble(in_shard, [spread_core(groups, size) for groups in in_second], size, shards)
    out_pieces, gate_up_pieces = after((jnp.stack(out_pieces), jnp.stack(gate_up_pieces)), w_in)
    rest_orders = (one, two, one, two)
    rest_first = [
        spread_first(piece, size, order)
        for piece, order in zip(
            (
                out_pieces[:, :out_piece_rows],
                out_pieces[:, out_piece_rows:],
                gate_up_pieces[:, :half_gate_up],
                gate_up_pieces[:, half_gate_up:],
            ),
            rest_orders,
        )
    ]
    query_width, pair_width = w_query.shape[1], key_value_weight.shape[1]
    attended_width = w_attn_out.shape[0] * shards
    in_width = query_width + pair_width + w_mixer_in.shape[1]

    item_count = rows.shape[0]
    index = jnp.arange(item_count, dtype=jnp.int32)
    live = (segments >= 0).astype(jnp.float32)[:, None]
    allowed = (segments[:, None] == segments[None, :]) & (index[:, None] >= index[None, :])
    position = positions_of(segments)
    same_seg = jnp.stack(
        [
            jnp.concatenate(
                [
                    jnp.zeros((offset,), jnp.float32),
                    (segments[offset:] == segments[: item_count - offset]).astype(jnp.float32),
                ]
            )
            for offset in range(KC)
        ]
    )
    wide = rows.astype(jnp.float32)
    wide_cot = cotangent.astype(jnp.float32)
    d_out = (live * wide_cot).astype(jnp.bfloat16)
    normed, pull_first = jax.vjp(rms_norm, wide, norm_gain)
    normed_b = normed.astype(jnp.bfloat16)
    projected = product(normed_b, w_in)
    query = projected[:, :query_width]
    key_value = projected[:, query_width : query_width + pair_width]
    inner_width = mixer_gain.shape[0]
    conv_width = conv_bias.shape[0]
    pair_end = query_width + pair_width
    gate_end = pair_end + inner_width
    gate_z = projected[:, pair_end:gate_end]
    conv_in = projected[:, gate_end : gate_end + conv_width]
    dt_raw = projected[:, gate_end + conv_width :]
    out_pair = send_columns(halve_columns(d_out, size), size)
    conv_out, pull_conv = jax.vjp(
        lambda *values: conv_core(*values, same_seg), conv_in, conv_weight, conv_bias
    )

    attended, pull_attention = jax.vjp(
        lambda *values: attention_core(*values, position, allowed), query, key_value
    )
    stacks, conv_out = together([stacked for stacked, _ in rest_first], conv_out)
    rest_second = [
        spread_second(stacked, offsets, size, order)
        for stacked, (_, offsets), order in zip(stacks, rest_first, rest_orders)
    ]
    mixed, pull_mixer = jax.vjp(
        lambda *values: mixer_core(*values, allowed),
        conv_out,
        gate_z,
        dt_raw,
        dt_bias,
        decay_log,
        skip_gain,
        mixer_gain,
    )
    arrived = [[part for part, _ in groups] for groups in rest_second]
    arrived, attended, mixed = together(arrived, attended, mixed)
    rest = [
        spread_core([(part, places) for part, (_, places) in zip(parts, groups)], size)
        for parts, groups in zip(arrived, rest_second)
    ]
    w_out = assemble(out_shard, rest[:1], size, shards)
    w_down = assemble(w_down, rest[1:2], size, shards)
    w_gate_up = assemble(w_gate_up, rest[2:], size, shards)
    branches = grouped(attended.astype(jnp.bfloat16), mixed.astype(jnp.bfloat16), shards)
    middle = wide + live * product(branches, w_out)
    normed2, pull_second = jax.vjp(rms_norm, middle, ffn_gain)
    normed2_b = normed2.astype(jnp.bfloat16)
    gate_up = product(normed2_b, w_gate_up)
    act, pull_act = jax.vjp(swiglu, gate_up)
    act_b = act.astype(jnp.bfloat16)
    early = send_rows(jnp.concatenate([normed_b, branches], axis=1), size)
    late = send_rows(jnp.concatenate([normed2_b, act_b], axis=1), size)

    (d_gate_up,) = pull_act(product_nt(d_out, w_down))
    d_gate_up = d_gate_up.astype(jnp.bfloat16)
    gate_up_half = halve_columns(d_gate_up, size)
    d_middle_norm, grad_ffn_gain = pull_second(product_nt(d_gate_up, w_gate_up))
    d_middle = wide_cot + d_middle_norm
    d_branch = (live * d_middle).astype(jnp.bfloat16)
    branch_half = halve_columns(d_branch, size)
    d_attended, d_mixed = ungrouped(product_nt(d_branch, w_out), attended_width, shards)
    gate_up_half, branch_half, early, d_attended, d_mixed = together(
        gate_up_half, branch_half, early, d_attended, d_mixed
    )
    gate_up_rights = send_columns(gate_up_half, size)
    branch_rights = send_columns(branch_half, size)
    early = pair_rows(early, size)
    d_query, d_keyval = pull_attention(d_attended)
    d_attention = jnp.concatenate([d_query.astype(jnp.bfloat16), d_keyval.astype(jnp.bfloat16)], axis=1)
    late, gate_up_rights, branch_rights, early, d_attention, d_mixed = together(
        late, gate_up_rights, branch_rights, early, d_attention, d_mixed
    )
    late = pair_rows(late, size)
    d_conv_out, d_gate_z, d_dt_raw, *d_small = pull_mixer(d_mixed)
    late, d_conv_out = together(late, d_conv_out)
    d_conv_in, *d_conv = pull_conv(d_conv_out)
    d_small = d_conv + d_small
    d_in = jnp.concatenate(
        [d_attention]
        + [part.astype(jnp.bfloat16) for part in (d_gate_z, d_conv_in, d_dt_raw)]
        + [jnp.zeros((item_count, -in_width % (size * LANES)), jnp.bfloat16)],
        axis=1,
    )
    in_rights = send_columns(halve_columns(d_in, size), size)
    d_input_norm, grad_norm_gain = pull_first(product_nt(d_in[:, :in_width], w_in))
    grad_input = d_middle + d_input_norm
    layer_output = (middle + live * product(act_b, w_down)).astype(jnp.bfloat16)

    model, hidden = normed_b.shape[1], act_b.shape[1]
    gu_width, width = d_gate_up.shape[1] // size, model // size
    part_rows = model // shards

    def folded(gradient):
        values = gradient.reshape(shards, -1, part_rows, width)
        return [values[:, i] for i in range(values.shape[1])]

    parts = jnp.concatenate(
        [
            column_gradient(late, gate_up_rights, 0, model).reshape(shards, part_rows, gu_width),
            *folded(column_gradient(late, out_pair, model, model + hidden)),
            *folded(column_gradient(early, branch_rights, model, model + branches.shape[1])),
        ],
        axis=2,
    )
    attended_rows = attended_width // shards
    out_rows = branches.shape[1] // shards
    down_rows = hidden // shards

    def pair_blocks(piece):
        own = jnp.stack(send_rows(piece, size))
        return own, swap(own, "rep", size, 1)

    def write_late(place, block, outs):
        gate_up_ref, down_ref, attended_ref, mixed_ref = outs
        gate_up_ref[:, place * gu_width : (place + 1) * gu_width] = block[:, :gu_width]
        columns = slice(place * width, (place + 1) * width)
        at = gu_width
        for row in range(0, down_rows, part_rows):
            down_ref[row : row + part_rows, columns] = block[:, at : at + width]
            at += width
        for row in range(0, out_rows, part_rows):
            values = block[:, at : at + width]
            at += width
            here = max(0, min(part_rows, attended_rows - row))
            if here:
                attended_ref[row : row + here, columns] = values[:here]
            if here < part_rows:
                start = row + here - attended_rows
                mixed_ref[start : start + part_rows - here, columns] = values[here:]

    late_own, late_near = pair_blocks(sum_of(send_shards(parts, shards)))
    grad_gate_up, grad_down, grad_attn_out, grad_mixer_out = unpack_columns(
        late_own,
        late_near,
        size,
        write_late,
        [
            (part_rows, d_gate_up.shape[1]),
            (down_rows, model),
            (attended_rows, model),
            (out_rows - attended_rows, model),
        ],
    )

    in_block = in_rights.shape[2]
    in_parts = column_gradient(early, in_rights, 0, model).reshape(shards, part_rows, in_block)

    def write_in(place, block, outs):
        start, stop = place * in_block, (place + 1) * in_block
        begin = 0
        for out_ref in outs:
            end = begin + out_ref.shape[1]
            low, high = max(start, begin), min(stop, end)
            if low < high:
                out_ref[:, low - begin : high - begin] = block[:, low - start : high - start]
            begin = end

    in_own, in_near = pair_blocks(sum_of(send_shards(in_parts, shards)))
    grad_query, grad_pair, grad_mixer_in = unpack_columns(
        in_own,
        in_near,
        size,
        write_in,
        [(part_rows, w.shape[1]) for w in (w_query, key_value_weight, w_mixer_in)],
    )
    small = (grad_norm_gain, *d_small, grad_ffn_gain)
    flat = jnp.concatenate([part.reshape(-1) for part in small])
    flat = jnp.pad(flat, (0, -flat.shape[0] % (8 * LANES))).reshape(-1, LANES)
    flat = total_of(flat, size, shards).reshape(-1)
    summed = []
    start = 0
    for part in small:
        summed.append(flat[start : start + part.size].reshape(part.shape))
        start += part.size
    return (
        layer_output,
        grad_input,
        summed[0],
        grad_query,
        grad_pair,
        grad_mixer_in,
        *summed[1:7],
        grad_mixer_out,
        grad_attn_out,
        summed[7],
        grad_gate_up,
        grad_down,
    )


def solution(mesh):
    return jax.shard_map(
        functools.partial(layer, mesh.shape["rep"], mesh.shape["shard"]),
        mesh=mesh,
        in_specs=(
            P(("rep", "shard"), None),
            P(("rep", "shard")),
            P(("rep", "shard"), None),
            P(),
            P("shard", None),
            P("shard", None),
            P("shard", None),
            P(),
            P(),
            P(),
            P(),
            P(),
            P(),
            P("shard", None),
            P("shard", None),
            P(),
            P("shard", None),
            P("shard", None),
        ),
        out_specs=(
            P(("rep", "shard"), None),
            P(("rep", "shard"), None),
            P(),
            P("shard", None),
            P("shard", None),
            P("shard", None),
            P(),
            P(),
            P(),
            P(),
            P(),
            P(),
            P("shard", None),
            P("shard", None),
            P(),
            P("shard", None),
            P("shard", None),
        ),
        check_vma=False,
    )
```

```python
import functools
import math

import jax
import jax.numpy as jnp
from jax import lax
from jax.experimental import pallas as pl
from jax.experimental.pallas import tpu as pltpu
from jax.sharding import PartitionSpec as P

FF = 2048
MH = 24
HEAD_SIZE = 64
NS = 128
KC = 4
QUERY_HEADS = 8
KEY_VALUE_HEADS = 2
DI = 1536
CONV = 1792


EPS = 1e-05
ROPE_BASE = 100000000000.0


def product(left, right):
    return jnp.dot(left, right, preferred_element_type=jnp.float32)


def product_tn(left, right):
    return lax.dot_general(
        left, right, (((0,), (0,)), ((), ())), preferred_element_type=jnp.float32
    )


def product_nt(left, right):
    return lax.dot_general(
        left, right, (((1,), (1,)), ((), ())), preferred_element_type=jnp.float32
    )


def rms_norm(values, gain):
    return values * lax.rsqrt(jnp.mean(values * values, axis=-1, keepdims=True) + EPS) * gain


def positions_of(segments):
    item_count = segments.shape[0]
    index = jnp.arange(item_count, dtype=jnp.int32)
    starts = jnp.concatenate([jnp.ones((1,), bool), segments[1:] != segments[:-1]])
    begin = lax.cummax(jnp.where(starts, index, 0), axis=0)
    return index - begin


def rotate(values, position):
    half = HEAD_SIZE // 2
    freqs = ROPE_BASE ** (-2.0 * jnp.arange(half, dtype=jnp.float32) / HEAD_SIZE)
    angles = position.astype(jnp.float32)[:, None] * freqs[None, :]
    cosine = jnp.cos(angles)[:, None, :]
    sine = jnp.sin(angles)[:, None, :]
    first = values[..., :half]
    second = values[..., half:]
    return jnp.concatenate(
        [first * cosine - second * sine, second * cosine + first * sine], axis=-1
    )


def silu(values):
    return values / (1.0 + jnp.exp(-values))


def attention_core(query, key_value, position, allowed):
    item_count = query.shape[0]
    heads_q = query.reshape(item_count, QUERY_HEADS, HEAD_SIZE)
    paired_items = key_value.reshape(item_count, 2, KEY_VALUE_HEADS, HEAD_SIZE)
    keys = rotate(paired_items[:, 0], position)
    values = paired_items[:, 1]
    heads_q = rotate(heads_q, position)
    shard_group = QUERY_HEADS // KEY_VALUE_HEADS
    keys = jnp.repeat(keys, shard_group, axis=1)
    values = jnp.repeat(values, shard_group, axis=1)
    scores = jnp.einsum("thd,shd->hts", heads_q, keys, precision=lax.Precision.HIGHEST) / math.sqrt(
        HEAD_SIZE
    )
    scores = jnp.where(allowed[None], scores, -jnp.inf)
    highest = jnp.max(scores, axis=-1, keepdims=True)
    expo = jnp.exp(scores - highest)
    probs = expo / jnp.sum(expo, axis=-1, keepdims=True)
    return jnp.einsum("hts,shd->thd", probs, values, precision=lax.Precision.HIGHEST).reshape(
        item_count, QUERY_HEADS * HEAD_SIZE
    )


def conv_core(conv_in, conv_weight, conv_bias, same_seg):
    item_count = conv_in.shape[0]
    total = jnp.zeros((item_count, CONV), jnp.float32) + conv_bias[None, :]
    for offset in range(KC):
        shifted = jnp.concatenate(
            [jnp.zeros((offset, CONV), jnp.float32), conv_in[: item_count - offset]], axis=0
        )
        total = total + conv_weight[KC - 1 - offset][None, :] * shifted * same_seg[offset][:, None]
    return silu(total)


def mixer_core(
    conv_out,
    gate_z,
    dt_raw,
    dt_bias,
    decay_log,
    skip_gain,
    mixer_gain,
    allowed,
):
    item_count = conv_out.shape[0]
    inner = conv_out[:, :DI].reshape(item_count, MH, HEAD_SIZE)
    bmat = conv_out[:, DI : DI + NS]
    cmat = conv_out[:, DI + NS :]
    step = jax.nn.softplus(dt_raw + dt_bias[None, :])
    csum = jnp.cumsum(step * (-jnp.exp(decay_log))[None, :], axis=0)
    gaps = csum[:, None, :] - csum[None, :, :]
    decay = jnp.exp(jnp.where(allowed[:, :, None], gaps, -jnp.inf))
    gram = jnp.dot(cmat, bmat.T, precision=lax.Precision.HIGHEST)
    mixing = gram[:, :, None] * decay * step[None, :, :]
    outputs = jnp.einsum("tsh,shp->thp", mixing, inner, precision=lax.Precision.HIGHEST)
    outputs = outputs + skip_gain[None, :, None] * inner
    gated = outputs.reshape(item_count, DI) * silu(gate_z)
    return rms_norm(gated, mixer_gain)


def swiglu(gate_up):
    return silu(gate_up[:, :FF]) * gate_up[:, FF:]


LANES = 128
SUBLANES = 8


def bit_count(size):
    return size.bit_length() - 1


def swap(values, axis_name, size, flip):
    return lax.ppermute(values, axis_name, [(i, i ^ flip) for i in range(size)])


def shift(values, axis_name, size, by):
    return lax.ppermute(values, axis_name, [(i, (i + by) % size) for i in range(size)])


def together(*values):
    return lax.optimization_barrier(values)


def after(values, done):
    return lax.optimization_barrier((values, done))[0]


def spread_first(piece, size, order):
    stacked, offsets = piece[None], [0]
    for bit in order[:-1]:
        stacked = jnp.concatenate([stacked, swap(stacked, "rep", size, 1 << bit)], axis=0)
        offsets = offsets + [offset ^ (1 << bit) for offset in offsets]
    return stacked, offsets


def spread_second(stacked, offsets, size, order):
    groups = [(stacked, offsets)]
    if order:
        flip = 1 << order[-1]
        groups.append((swap(stacked, "rep", size, flip), [offset ^ flip for offset in offsets]))
    return groups


def spread_core(groups, size):
    return groups + [
        (swap(part, "rep", size, 1), [place ^ 1 for place in places]) for part, places in groups
    ]


def spread(piece, size, order):
    return spread_core(spread_second(*spread_first(piece, size, order), size, order), size)


def assemble(shard, halves, size, shards):
    rows, width = shard.shape
    piece = rows // size
    half = piece // len(halves)

    def copies(me, own):
        yield own * rows, None, None, None, None
        for which, groups in enumerate(halves):
            for part, (_, places) in enumerate(groups):
                for slot, place in enumerate(places):
                    for step in range(1, shards):
                        owner = (own + (shards - step)) % shards
                        start = owner * rows + (me ^ place) * piece + which * half
                        yield start, which, part, slot, step - 1

    flat = [part for groups in halves for part, _ in groups]
    per_half = len(halves[0])
    if half % SUBLANES != 0:
        own = lax.axis_index("shard")
        whole = jnp.zeros((rows * shards, width), shard.dtype)
        for start, which, part, slot, step in copies(lax.axis_index("rep"), own):
            block = shard if which is None else flat[which * per_half + part][slot, step]
            whole = lax.dynamic_update_slice_in_dim(whole, block, start, axis=0)
        return whole

    def kernel(own_ref, *refs):
        *parts, whole_ref = refs
        me, own = lax.axis_index("rep"), lax.axis_index("shard")
        for start, which, part, slot, step in copies(me, own):
            start = pl.multiple_of(start, SUBLANES)
            if which is None:
                whole_ref[pl.ds(start, rows), :] = own_ref[...]
            else:
                whole_ref[pl.ds(start, half), :] = parts[which * per_half + part][slot, step]

    return pl.pallas_call(
        kernel,
        out_shape=jax.ShapeDtypeStruct((rows * shards, width), shard.dtype),
        in_specs=[pl.BlockSpec(memory_space=pltpu.VMEM)] * (1 + len(flat)),
        out_specs=pl.BlockSpec(memory_space=pltpu.VMEM),
    )(shard, *flat)


def ring_step(piece, shards):
    return shift(piece, "shard", shards, 1)


def own_piece(shard, size):
    rows = shard.shape[0] // size
    return lax.dynamic_slice_in_dim(shard, lax.axis_index("rep") * rows, rows, axis=0)


def outer_offsets(size):
    return [offset << 1 for offset in range(size // 2)]


def send_rows(rows, size):
    return [rows if offset == 0 else swap(rows, "rep", size, offset) for offset in outer_offsets(size)]


def pair_rows(parts, size):
    rows = jnp.concatenate(parts, axis=0)
    return rows, swap(rows, "rep", size, 1)


def halve_columns(rows, size):
    half = rows.shape[1] // 2
    mine = (lax.axis_index("rep") & 1) * half
    kept = lax.dynamic_slice_in_dim(rows, mine, half, axis=1)
    sent = lax.dynamic_slice_in_dim(rows, half - mine, half, axis=1)
    return jnp.stack([kept, swap(sent, "rep", size, 1)])


def send_columns(pair, size):
    width = pair.shape[2] // (size // 2)
    parts = []
    for offset in outer_offsets(size):
        target = (lax.axis_index("rep") ^ offset) >> 1
        part = lax.dynamic_slice_in_dim(pair, target * width, width, axis=2)
        parts.append(part if offset == 0 else swap(part, "rep", size, offset))
    return jnp.concatenate(parts, axis=1)


def column_gradient(lefts, rights, start, stop):
    return sum(
        product_tn(left[:, start:stop], right) for left, right in zip(lefts, (rights[0], rights[1]))
    ).astype(jnp.bfloat16)


def send_shards(parts, shards):
    own = lax.axis_index("shard")

    def part_of(place):
        return lax.dynamic_index_in_dim(parts, place, axis=0, keepdims=False)

    return [part_of(own)] + [
        shift(part_of((own + step) % shards), "shard", shards, step) for step in range(1, shards)
    ]


def sum_of(parts):
    return sum(part.astype(jnp.float32) for part in parts).astype(jnp.bfloat16)


def unpack_columns(own, near, size, write, out_shapes):
    half = size // 2

    def kernel(*refs):
        if near is None:
            own_ref, *outs = refs
        else:
            own_ref, near_ref, *outs = refs
        member = lax.axis_index("rep")
        for place in range(size):
            if near is None:
                block = own_ref[(place % half) * 2 + place // half].astype(jnp.float32)
            else:
                slot = (member >> 1) ^ (place % half)
                same = (member & 1) == place // half
                block = jnp.where(
                    same, own_ref[slot].astype(jnp.float32), near_ref[slot].astype(jnp.float32)
                )
            write(place, block, outs)

    arrays = (own,) if near is None else (own, near)
    return pl.pallas_call(
        kernel,
        out_shape=[jax.ShapeDtypeStruct(shape, jnp.float32) for shape in out_shapes],
        in_specs=[pl.BlockSpec(memory_space=pltpu.VMEM)] * len(arrays),
        out_specs=[pl.BlockSpec(memory_space=pltpu.VMEM)] * len(out_shapes),
    )(*arrays)


def total_of(values, size, shards):
    for bit in range(bit_count(size)):
        values = values + swap(values, "rep", size, 1 << bit)
    for bit in range(bit_count(shards)):
        values = values + swap(values, "shard", shards, 1 << bit)
    return values


def grouped(first, second, shards):
    one, two = first.shape[1] // shards, second.shape[1] // shards
    parts = []
    for i in range(shards):
        parts += [first[:, i * one : (i + 1) * one], second[:, i * two : (i + 1) * two]]
    return jnp.concatenate(parts, axis=1)


def ungrouped(values, first, shards):
    one, both = first // shards, values.shape[1] // shards
    starts = range(0, values.shape[1], both)
    return (
        jnp.concatenate([values[:, start : start + one] for start in starts], axis=1),
        jnp.concatenate([values[:, start + one : start + both] for start in starts], axis=1),
    )


def layer(
    size,
    shards,
    rows,
    segments,
    cotangent,
    norm_gain,
    w_query,
    key_value_weight,
    w_mixer_in,
    conv_weight,
    conv_bias,
    dt_bias,
    decay_log,
    skip_gain,
    mixer_gain,
    w_mixer_out,
    w_attn_out,
    ffn_gain,
    w_gate_up,
    w_down,
):
    one = list(range(1, bit_count(size)))
    two = one[::-1]
    in_shard = jnp.concatenate([w_query, key_value_weight, w_mixer_in], axis=1)
    out_shard = jnp.concatenate([w_attn_out, w_mixer_out], axis=0)
    half_in = in_shard.shape[0] // size // 2
    in_piece = jnp.concatenate(
        [own_piece(w, size) for w in (w_query, key_value_weight, w_mixer_in)], axis=1
    )
    in_pieces = []
    for _ in range(1, shards):
        in_piece = ring_step(in_piece, shards)
        in_pieces.append(in_piece)
    in_pieces = jnp.stack(in_pieces)
    in_first = [
        spread_first(in_pieces[:, :half_in], size, one),
        spread_first(in_pieces[:, half_in:], size, two),
    ]
    in_second = [
        spread_second(*in_first[0], size, one),
        spread_second(*in_first[1], size, two),
    ]
    w_in = assemble(in_shard, [spread_core(groups, size) for groups in in_second], size, shards)
    model = rows.shape[1]
    blocks = w_gate_up.shape[1] // model
    rest = (own_piece(out_shard, size), own_piece(w_down, size), own_piece(w_gate_up, size))
    ends = [0, rest[0].shape[0], rest[0].shape[0] + rest[1].shape[0]]
    gate_up_rows = rest[2].shape[0]
    rest = jnp.concatenate(
        list(rest[:2]) + [rest[2][:, i * model : (i + 1) * model] for i in range(blocks)], axis=0
    )
    rest = lax.all_gather(rest, ("shard", "rep"), axis=0)

    def rest_rows(start, stop):
        return rest[:, start:stop].reshape(-1, model)

    w_out = rest_rows(ends[0], ends[1])
    w_down = rest_rows(ends[1], ends[2])
    w_gate_up = jnp.concatenate(
        [
            rest_rows(ends[2] + i * gate_up_rows, ends[2] + (i + 1) * gate_up_rows)
            for i in range(blocks)
        ],
        axis=1,
    )
    query_width, pair_width = w_query.shape[1], key_value_weight.shape[1]
    attended_width = w_attn_out.shape[0] * shards
    in_width = query_width + pair_width + w_mixer_in.shape[1]

    item_count = rows.shape[0]
    index = jnp.arange(item_count, dtype=jnp.int32)
    live = (segments >= 0).astype(jnp.float32)[:, None]
    allowed = (segments[:, None] == segments[None, :]) & (index[:, None] >= index[None, :])
    position = positions_of(segments)
    same_seg = jnp.stack(
        [
            jnp.concatenate(
                [
                    jnp.zeros((offset,), jnp.float32),
                    (segments[offset:] == segments[: item_count - offset]).astype(jnp.float32),
                ]
            )
            for offset in range(KC)
        ]
    )
    wide = rows.astype(jnp.float32)
    wide_cot = cotangent.astype(jnp.float32)
    d_out = (live * wide_cot).astype(jnp.bfloat16)
    normed, pull_first = jax.vjp(rms_norm, wide, norm_gain)
    normed_b = normed.astype(jnp.bfloat16)
    projected = product(normed_b, w_in)
    query = projected[:, :query_width]
    key_value = projected[:, query_width : query_width + pair_width]
    inner_width = mixer_gain.shape[0]
    conv_width = conv_bias.shape[0]
    pair_end = query_width + pair_width
    gate_end = pair_end + inner_width
    gate_z = projected[:, pair_end:gate_end]
    conv_in = projected[:, gate_end : gate_end + conv_width]
    dt_raw = projected[:, gate_end + conv_width :]
    out_pair = send_columns(halve_columns(d_out, size), size)
    conv_out, pull_conv = jax.vjp(
        lambda *values: conv_core(*values, same_seg), conv_in, conv_weight, conv_bias
    )

    attended, pull_attention = jax.vjp(
        lambda *values: attention_core(*values, position, allowed), query, key_value
    )
    mixed, pull_mixer = jax.vjp(
        lambda *values: mixer_core(*values, allowed),
        conv_out,
        gate_z,
        dt_raw,
        dt_bias,
        decay_log,
        skip_gain,
        mixer_gain,
    )
    branches = grouped(attended.astype(jnp.bfloat16), mixed.astype(jnp.bfloat16), shards)
    middle = wide + live * product(branches, w_out)
    normed2, pull_second = jax.vjp(rms_norm, middle, ffn_gain)
    normed2_b = normed2.astype(jnp.bfloat16)
    gate_up = product(normed2_b, w_gate_up)
    act, pull_act = jax.vjp(swiglu, gate_up)
    act_b = act.astype(jnp.bfloat16)
    early = send_rows(jnp.concatenate([normed_b, branches], axis=1), size)
    late = send_rows(jnp.concatenate([normed2_b, act_b], axis=1), size)

    (d_gate_up,) = pull_act(product_nt(d_out, w_down))
    d_gate_up = d_gate_up.astype(jnp.bfloat16)
    gate_up_half = halve_columns(d_gate_up, size)
    d_middle_norm, grad_ffn_gain = pull_second(product_nt(d_gate_up, w_gate_up))
    d_middle = wide_cot + d_middle_norm
    d_branch = (live * d_middle).astype(jnp.bfloat16)
    branch_half = halve_columns(d_branch, size)
    d_attended, d_mixed = ungrouped(product_nt(d_branch, w_out), attended_width, shards)
    gate_up_half, branch_half, early, d_attended, d_mixed = together(
        gate_up_half, branch_half, early, d_attended, d_mixed
    )
    gate_up_rights = send_columns(gate_up_half, size)
    branch_rights = send_columns(branch_half, size)
    early = pair_rows(early, size)
    d_query, d_keyval = pull_attention(d_attended)
    d_attention = jnp.concatenate([d_query.astype(jnp.bfloat16), d_keyval.astype(jnp.bfloat16)], axis=1)
    late, gate_up_rights, branch_rights, early, d_attention, d_mixed = together(
        late, gate_up_rights, branch_rights, early, d_attention, d_mixed
    )
    late = pair_rows(late, size)
    d_conv_out, d_gate_z, d_dt_raw, *d_small = pull_mixer(d_mixed)
    late, d_conv_out = together(late, d_conv_out)
    d_conv_in, *d_conv = pull_conv(d_conv_out)
    d_small = d_conv + d_small
    d_in = jnp.concatenate(
        [d_attention]
        + [part.astype(jnp.bfloat16) for part in (d_gate_z, d_conv_in, d_dt_raw)]
        + [jnp.zeros((item_count, -in_width % (size * LANES)), jnp.bfloat16)],
        axis=1,
    )
    in_rights = send_columns(halve_columns(d_in, size), size)
    d_input_norm, grad_norm_gain = pull_first(product_nt(d_in[:, :in_width], w_in))
    grad_input = d_middle + d_input_norm
    layer_output = (middle + live * product(act_b, w_down)).astype(jnp.bfloat16)

    model, hidden = normed_b.shape[1], act_b.shape[1]
    gu_width, width = d_gate_up.shape[1] // size, model // size
    part_rows = model // shards

    def folded(gradient):
        values = gradient.reshape(shards, -1, part_rows, width)
        return [values[:, i] for i in range(values.shape[1])]

    parts = jnp.concatenate(
        [
            column_gradient(late, gate_up_rights, 0, model).reshape(shards, part_rows, gu_width),
            *folded(column_gradient(late, out_pair, model, model + hidden)),
            *folded(column_gradient(early, branch_rights, model, model + branches.shape[1])),
        ],
        axis=2,
    )
    attended_rows = attended_width // shards
    out_rows = branches.shape[1] // shards
    down_rows = hidden // shards

    def pair_blocks(piece):
        own = jnp.stack(send_rows(piece, size))
        return own, swap(own, "rep", size, 1)

    def write_late(place, block, outs):
        gate_up_ref, down_ref, attended_ref, mixed_ref = outs
        gate_up_ref[:, place * gu_width : (place + 1) * gu_width] = block[:, :gu_width]
        columns = slice(place * width, (place + 1) * width)
        at = gu_width
        for row in range(0, down_rows, part_rows):
            down_ref[row : row + part_rows, columns] = block[:, at : at + width]
            at += width
        for row in range(0, out_rows, part_rows):
            values = block[:, at : at + width]
            at += width
            here = max(0, min(part_rows, attended_rows - row))
            if here:
                attended_ref[row : row + here, columns] = values[:here]
            if here < part_rows:
                start = row + here - attended_rows
                mixed_ref[start : start + part_rows - here, columns] = values[here:]

    late_piece = lax.psum_scatter(parts, "shard", scatter_dimension=0, tiled=False)
    late_blocks = lax.all_gather(late_piece, "rep", axis=0)
    grad_gate_up, grad_down, grad_attn_out, grad_mixer_out = unpack_columns(
        late_blocks,
        None,
        size,
        write_late,
        [
            (part_rows, d_gate_up.shape[1]),
            (down_rows, model),
            (attended_rows, model),
            (out_rows - attended_rows, model),
        ],
    )

    in_block = in_rights.shape[2]
    in_parts = column_gradient(early, in_rights, 0, model).reshape(shards, part_rows, in_block)

    def write_in(place, block, outs):
        start, stop = place * in_block, (place + 1) * in_block
        begin = 0
        for out_ref in outs:
            end = begin + out_ref.shape[1]
            low, high = max(start, begin), min(stop, end)
            if low < high:
                out_ref[:, low - begin : high - begin] = block[:, low - start : high - start]
            begin = end

    in_own, in_near = pair_blocks(sum_of(send_shards(in_parts, shards)))
    grad_query, grad_pair, grad_mixer_in = unpack_columns(
        in_own,
        in_near,
        size,
        write_in,
        [(part_rows, w.shape[1]) for w in (w_query, key_value_weight, w_mixer_in)],
    )
    small = (grad_norm_gain, *d_small, grad_ffn_gain)
    flat = jnp.concatenate([part.reshape(-1) for part in small])
    flat = jnp.pad(flat, (0, -flat.shape[0] % (8 * LANES))).reshape(-1, LANES)
    flat = total_of(flat, size, shards).reshape(-1)
    summed = []
    start = 0
    for part in small:
        summed.append(flat[start : start + part.size].reshape(part.shape))
        start += part.size
    return (
        layer_output,
        grad_input,
        summed[0],
        grad_query,
        grad_pair,
        grad_mixer_in,
        *summed[1:7],
        grad_mixer_out,
        grad_attn_out,
        summed[7],
        grad_gate_up,
        grad_down,
    )


def solution(mesh):
    return jax.shard_map(
        functools.partial(layer, mesh.shape["rep"], mesh.shape["shard"]),
        mesh=mesh,
        in_specs=(
            P(("rep", "shard"), None),
            P(("rep", "shard")),
            P(("rep", "shard"), None),
            P(),
            P("shard", None),
            P("shard", None),
            P("shard", None),
            P(),
            P(),
            P(),
            P(),
            P(),
            P(),
            P("shard", None),
            P("shard", None),
            P(),
            P("shard", None),
            P("shard", None),
        ),
        out_specs=(
            P(("rep", "shard"), None),
            P(("rep", "shard"), None),
            P(),
            P("shard", None),
            P("shard", None),
            P("shard", None),
            P(),
            P(),
            P(),
            P(),
            P(),
            P(),
            P("shard", None),
            P("shard", None),
            P(),
            P("shard", None),
            P("shard", None),
        ),
        check_vma=False,
    )
```

```python
import functools
import math

import jax
import jax.numpy as jnp
from jax import lax
from jax.experimental import pallas as pl
from jax.experimental.pallas import tpu as pltpu
from jax.sharding import PartitionSpec as P

FF = 2048
MH = 24
HEAD_SIZE = 64
NS = 128
KC = 4
QUERY_HEADS = 8
KEY_VALUE_HEADS = 2
DI = 1536
CONV = 1792


EPS = 1e-05
ROPE_BASE = 100000000000.0


def product(left, right):
    return jnp.dot(left, right, preferred_element_type=jnp.float32)


def product_tn(left, right):
    return lax.dot_general(
        left, right, (((0,), (0,)), ((), ())), preferred_element_type=jnp.float32
    )


def product_nt(left, right):
    return lax.dot_general(
        left, right, (((1,), (1,)), ((), ())), preferred_element_type=jnp.float32
    )


def rms_norm(values, gain):
    return values * lax.rsqrt(jnp.mean(values * values, axis=-1, keepdims=True) + EPS) * gain


def positions_of(segments):
    item_count = segments.shape[0]
    index = jnp.arange(item_count, dtype=jnp.int32)
    starts = jnp.concatenate([jnp.ones((1,), bool), segments[1:] != segments[:-1]])
    begin = lax.cummax(jnp.where(starts, index, 0), axis=0)
    return index - begin


def rotate(values, position):
    half = HEAD_SIZE // 2
    freqs = ROPE_BASE ** (-2.0 * jnp.arange(half, dtype=jnp.float32) / HEAD_SIZE)
    angles = position.astype(jnp.float32)[:, None] * freqs[None, :]
    cosine = jnp.cos(angles)[:, None, :]
    sine = jnp.sin(angles)[:, None, :]
    first = values[..., :half]
    second = values[..., half:]
    return jnp.concatenate(
        [first * cosine - second * sine, second * cosine + first * sine], axis=-1
    )


def silu(values):
    return values / (1.0 + jnp.exp(-values))


def attention_core(query, key_value, position, allowed):
    item_count = query.shape[0]
    heads_q = query.reshape(item_count, QUERY_HEADS, HEAD_SIZE)
    paired_items = key_value.reshape(item_count, 2, KEY_VALUE_HEADS, HEAD_SIZE)
    keys = rotate(paired_items[:, 0], position)
    values = paired_items[:, 1]
    heads_q = rotate(heads_q, position)
    shard_group = QUERY_HEADS // KEY_VALUE_HEADS
    keys = jnp.repeat(keys, shard_group, axis=1)
    values = jnp.repeat(values, shard_group, axis=1)
    scores = jnp.einsum("thd,shd->hts", heads_q, keys, precision=lax.Precision.HIGHEST) / math.sqrt(
        HEAD_SIZE
    )
    scores = jnp.where(allowed[None], scores, -jnp.inf)
    highest = jnp.max(scores, axis=-1, keepdims=True)
    expo = jnp.exp(scores - highest)
    probs = expo / jnp.sum(expo, axis=-1, keepdims=True)
    return jnp.einsum("hts,shd->thd", probs, values, precision=lax.Precision.HIGHEST).reshape(
        item_count, QUERY_HEADS * HEAD_SIZE
    )


def conv_core(conv_in, conv_weight, conv_bias, same_seg):
    item_count = conv_in.shape[0]
    total = jnp.zeros((item_count, CONV), jnp.float32) + conv_bias[None, :]
    for offset in range(KC):
        shifted = jnp.concatenate(
            [jnp.zeros((offset, CONV), jnp.float32), conv_in[: item_count - offset]], axis=0
        )
        total = total + conv_weight[KC - 1 - offset][None, :] * shifted * same_seg[offset][:, None]
    return silu(total)


def mixer_core(
    conv_out,
    gate_z,
    dt_raw,
    dt_bias,
    decay_log,
    skip_gain,
    mixer_gain,
    allowed,
):
    item_count = conv_out.shape[0]
    inner = conv_out[:, :DI].reshape(item_count, MH, HEAD_SIZE)
    bmat = conv_out[:, DI : DI + NS]
    cmat = conv_out[:, DI + NS :]
    step = jax.nn.softplus(dt_raw + dt_bias[None, :])
    csum = jnp.cumsum(step * (-jnp.exp(decay_log))[None, :], axis=0)
    gaps = csum[:, None, :] - csum[None, :, :]
    decay = jnp.exp(jnp.where(allowed[:, :, None], gaps, -jnp.inf))
    gram = jnp.dot(cmat, bmat.T, precision=lax.Precision.HIGHEST)
    mixing = gram[:, :, None] * decay * step[None, :, :]
    outputs = jnp.einsum("tsh,shp->thp", mixing, inner, precision=lax.Precision.HIGHEST)
    outputs = outputs + skip_gain[None, :, None] * inner
    gated = outputs.reshape(item_count, DI) * silu(gate_z)
    return rms_norm(gated, mixer_gain)


def swiglu(gate_up):
    return silu(gate_up[:, :FF]) * gate_up[:, FF:]


LANES = 128
SUBLANES = 8


def bit_count(size):
    return size.bit_length() - 1


def swap(values, axis_name, size, flip):
    return lax.ppermute(values, axis_name, [(i, i ^ flip) for i in range(size)])


def shift(values, axis_name, size, by):
    return lax.ppermute(values, axis_name, [(i, (i + by) % size) for i in range(size)])


def together(*values):
    return lax.optimization_barrier(values)


def after(values, done):
    return lax.optimization_barrier((values, done))[0]


def spread_first(piece, size, order):
    stacked, offsets = piece[None], [0]
    for bit in order[:-1]:
        stacked = jnp.concatenate([stacked, swap(stacked, "rep", size, 1 << bit)], axis=0)
        offsets = offsets + [offset ^ (1 << bit) for offset in offsets]
    return stacked, offsets


def spread_second(stacked, offsets, size, order):
    groups = [(stacked, offsets)]
    if order:
        flip = 1 << order[-1]
        groups.append((swap(stacked, "rep", size, flip), [offset ^ flip for offset in offsets]))
    return groups


def spread_core(groups, size):
    return groups + [
        (swap(part, "rep", size, 1), [place ^ 1 for place in places]) for part, places in groups
    ]


def spread(piece, size, order):
    return spread_core(spread_second(*spread_first(piece, size, order), size, order), size)


def assemble(shard, halves, size, shards):
    rows, width = shard.shape
    piece = rows // size
    half = piece // len(halves)

    def copies(me, own):
        yield own * rows, None, None, None, None
        for which, groups in enumerate(halves):
            for part, (_, places) in enumerate(groups):
                for slot, place in enumerate(places):
                    for step in range(1, shards):
                        owner = (own + (shards - step)) % shards
                        start = owner * rows + (me ^ place) * piece + which * half
                        yield start, which, part, slot, step - 1

    flat = [part for groups in halves for part, _ in groups]
    per_half = len(halves[0])
    if half % SUBLANES != 0:
        own = lax.axis_index("shard")
        whole = jnp.zeros((rows * shards, width), shard.dtype)
        for start, which, part, slot, step in copies(lax.axis_index("rep"), own):
            block = shard if which is None else flat[which * per_half + part][slot, step]
            whole = lax.dynamic_update_slice_in_dim(whole, block, start, axis=0)
        return whole

    def kernel(own_ref, *refs):
        *parts, whole_ref = refs
        me, own = lax.axis_index("rep"), lax.axis_index("shard")
        for start, which, part, slot, step in copies(me, own):
            start = pl.multiple_of(start, SUBLANES)
            if which is None:
                whole_ref[pl.ds(start, rows), :] = own_ref[...]
            else:
                whole_ref[pl.ds(start, half), :] = parts[which * per_half + part][slot, step]

    return pl.pallas_call(
        kernel,
        out_shape=jax.ShapeDtypeStruct((rows * shards, width), shard.dtype),
        in_specs=[pl.BlockSpec(memory_space=pltpu.VMEM)] * (1 + len(flat)),
        out_specs=pl.BlockSpec(memory_space=pltpu.VMEM),
    )(shard, *flat)


def ring_step(piece, shards):
    return shift(piece, "shard", shards, 1)


def own_piece(shard, size):
    rows = shard.shape[0] // size
    return lax.dynamic_slice_in_dim(shard, lax.axis_index("rep") * rows, rows, axis=0)


def outer_offsets(size):
    return [offset << 1 for offset in range(size // 2)]


def send_rows(rows, size):
    return [rows if offset == 0 else swap(rows, "rep", size, offset) for offset in outer_offsets(size)]


def halve_columns(rows, size):
    half = rows.shape[1] // 2
    mine = (lax.axis_index("rep") & 1) * half
    kept = lax.dynamic_slice_in_dim(rows, mine, half, axis=1)
    sent = lax.dynamic_slice_in_dim(rows, half - mine, half, axis=1)
    return jnp.stack([kept, swap(sent, "rep", size, 1)])


def send_columns(pair, size):
    width = pair.shape[2] // (size // 2)
    parts = []
    for offset in outer_offsets(size):
        target = (lax.axis_index("rep") ^ offset) >> 1
        part = lax.dynamic_slice_in_dim(pair, target * width, width, axis=2)
        parts.append(part if offset == 0 else swap(part, "rep", size, offset))
    item_count = pair.shape[1]

    def kernel(*refs):
        *part_refs, out_ref = refs
        member = lax.axis_index("rep")
        for offset, part_ref in zip(outer_offsets(size), part_refs):
            for bit in range(2):
                start = pl.multiple_of((member ^ offset ^ bit) * item_count, SUBLANES)
                out_ref[pl.ds(start, item_count), :] = part_ref[bit]

    return pl.pallas_call(
        kernel,
        out_shape=jax.ShapeDtypeStruct((size * item_count, width), pair.dtype),
        in_specs=[pl.BlockSpec(memory_space=pltpu.VMEM)] * len(parts),
        out_specs=pl.BlockSpec(memory_space=pltpu.VMEM),
    )(*parts)


def column_gradient(lefts, rights, start, stop):
    return product_tn(lefts[:, start:stop], rights).astype(jnp.bfloat16)


def send_shards(parts, shards):
    own = lax.axis_index("shard")

    def part_of(place):
        return lax.dynamic_index_in_dim(parts, place, axis=0, keepdims=False)

    return [part_of(own)] + [
        shift(part_of((own + step) % shards), "shard", shards, step) for step in range(1, shards)
    ]


def sum_of(parts):
    return sum(part.astype(jnp.float32) for part in parts).astype(jnp.bfloat16)


def unpack_columns(own, near, size, write, out_shapes):
    half = size // 2

    def kernel(*refs):
        if near is None:
            own_ref, *outs = refs
        else:
            own_ref, near_ref, *outs = refs
        member = lax.axis_index("rep")
        for place in range(size):
            if near is None:
                block = own_ref[(place % half) * 2 + place // half].astype(jnp.float32)
            else:
                slot = (member >> 1) ^ (place % half)
                same = (member & 1) == place // half
                block = jnp.where(
                    same, own_ref[slot].astype(jnp.float32), near_ref[slot].astype(jnp.float32)
                )
            write(place, block, outs)

    arrays = (own,) if near is None else (own, near)
    return pl.pallas_call(
        kernel,
        out_shape=[jax.ShapeDtypeStruct(shape, jnp.float32) for shape in out_shapes],
        in_specs=[pl.BlockSpec(memory_space=pltpu.VMEM)] * len(arrays),
        out_specs=[pl.BlockSpec(memory_space=pltpu.VMEM)] * len(out_shapes),
    )(*arrays)


def total_of(values, axis_name, size):
    for bit in range(bit_count(size)):
        values = values + swap(values, axis_name, size, 1 << bit)
    return values


def layer(
    size,
    shards,
    rows,
    segments,
    cotangent,
    norm_gain,
    w_query,
    key_value_weight,
    w_mixer_in,
    conv_weight,
    conv_bias,
    dt_bias,
    decay_log,
    skip_gain,
    mixer_gain,
    w_mixer_out,
    w_attn_out,
    ffn_gain,
    w_gate_up,
    w_down,
):
    one = list(range(1, bit_count(size)))
    two = one[::-1]
    in_shard = jnp.concatenate([w_query, key_value_weight, w_mixer_in], axis=1)
    half_in = in_shard.shape[0] // size // 2
    in_piece = jnp.concatenate(
        [own_piece(w, size) for w in (w_query, key_value_weight, w_mixer_in)], axis=1
    )
    in_pieces = []
    first_piece = in_piece
    for _ in range(1, shards):
        in_piece = ring_step(in_piece, shards)
        in_pieces.append(in_piece)
    in_pieces = jnp.stack(in_pieces)
    in_first = [
        spread_first(in_pieces[:, :half_in], size, one),
        spread_first(in_pieces[:, half_in:], size, two),
    ]
    in_second = [
        spread_second(*in_first[0], size, one),
        spread_second(*in_first[1], size, two),
    ]
    w_in = assemble(in_shard, [spread_core(groups, size) for groups in in_second], size, shards)
    model = rows.shape[1]
    blocks = w_gate_up.shape[1] // model
    rest = [own_piece(w, size) for w in (w_attn_out, w_mixer_out, w_down)]
    gate_up_piece = own_piece(w_gate_up, size)
    rest += [gate_up_piece[:, i * model : (i + 1) * model] for i in range(blocks)]
    ends = [0]
    for piece in rest:
        ends.append(ends[-1] + piece.shape[0])
    rest = lax.all_gather(after(jnp.concatenate(rest, axis=0), first_piece), ("shard", "rep"), axis=0)
    w_attn, w_mix, w_down, *gate_up_blocks = [
        rest[:, start:stop].reshape(-1, model) for start, stop in zip(ends, ends[1:])
    ]
    w_gate_up = jnp.concatenate(gate_up_blocks, axis=1)
    query_width, pair_width = w_query.shape[1], key_value_weight.shape[1]
    in_width = query_width + pair_width + w_mixer_in.shape[1]

    item_count = rows.shape[0]
    index = jnp.arange(item_count, dtype=jnp.int32)
    live = (segments >= 0).astype(jnp.float32)[:, None]
    allowed = (segments[:, None] == segments[None, :]) & (index[:, None] >= index[None, :])
    position = positions_of(segments)
    same_seg = jnp.stack(
        [
            jnp.concatenate(
                [
                    jnp.zeros((offset,), jnp.float32),
                    (segments[offset:] == segments[: item_count - offset]).astype(jnp.float32),
                ]
            )
            for offset in range(KC)
        ]
    )
    wide = rows.astype(jnp.float32)
    wide_cot = cotangent.astype(jnp.float32)
    d_out = (live * wide_cot).astype(jnp.bfloat16)
    normed, pull_first = jax.vjp(rms_norm, wide, norm_gain)
    normed_b = normed.astype(jnp.bfloat16)
    projected = product(normed_b, w_in)
    query = projected[:, :query_width]
    key_value = projected[:, query_width : query_width + pair_width]
    inner_width = mixer_gain.shape[0]
    conv_width = conv_bias.shape[0]
    pair_end = query_width + pair_width
    gate_end = pair_end + inner_width
    gate_z = projected[:, pair_end:gate_end]
    conv_in = projected[:, gate_end : gate_end + conv_width]
    dt_raw = projected[:, gate_end + conv_width :]
    out_pair = send_columns(halve_columns(d_out, size), size)
    conv_out, pull_conv = jax.vjp(
        lambda *values: conv_core(*values, same_seg), conv_in, conv_weight, conv_bias
    )

    attended, pull_attention = jax.vjp(
        lambda *values: attention_core(*values, position, allowed), query, key_value
    )
    mixed, pull_mixer = jax.vjp(
        lambda *values: mixer_core(*values, allowed),
        conv_out,
        gate_z,
        dt_raw,
        dt_bias,
        decay_log,
        skip_gain,
        mixer_gain,
    )
    attended_b = attended.astype(jnp.bfloat16)
    mixed_b = mixed.astype(jnp.bfloat16)
    middle = wide + live * (product(attended_b, w_attn) + product(mixed_b, w_mix))
    normed2, pull_second = jax.vjp(rms_norm, middle, ffn_gain)
    normed2_b = normed2.astype(jnp.bfloat16)
    gate_up = product(normed2_b, w_gate_up)
    act, pull_act = jax.vjp(swiglu, gate_up)
    act_b = act.astype(jnp.bfloat16)
    early = lax.all_gather(
        jnp.concatenate([normed_b, attended_b, mixed_b], axis=1), "rep", axis=0, tiled=True
    )
    late = lax.all_gather(jnp.concatenate([normed2_b, act_b], axis=1), "rep", axis=0, tiled=True)

    (d_gate_up,) = pull_act(product_nt(d_out, w_down))
    d_gate_up = d_gate_up.astype(jnp.bfloat16)
    gate_up_half = halve_columns(d_gate_up, size)
    d_middle_norm, grad_ffn_gain = pull_second(product_nt(d_gate_up, w_gate_up))
    d_middle = wide_cot + d_middle_norm
    d_branch = (live * d_middle).astype(jnp.bfloat16)
    branch_half = halve_columns(d_branch, size)
    d_attended = product_nt(d_branch, w_attn)
    d_mixed = product_nt(d_branch, w_mix)
    gate_up_half, branch_half, d_attended, d_mixed = together(
        gate_up_half, branch_half, d_attended, d_mixed
    )
    gate_up_rights = send_columns(gate_up_half, size)
    branch_rights = send_columns(branch_half, size)
    d_query, d_keyval = pull_attention(d_attended)
    d_attention = jnp.concatenate([d_query.astype(jnp.bfloat16), d_keyval.astype(jnp.bfloat16)], axis=1)
    gate_up_rights, branch_rights, d_attention, d_mixed = together(
        gate_up_rights, branch_rights, d_attention, d_mixed
    )
    d_conv_out, d_gate_z, d_dt_raw, *d_small = pull_mixer(d_mixed)
    late = after(late, d_conv_out)
    d_conv_in, *d_conv = pull_conv(d_conv_out)
    d_small = d_conv + d_small
    d_in = jnp.concatenate(
        [d_attention]
        + [part.astype(jnp.bfloat16) for part in (d_gate_z, d_conv_in, d_dt_raw)]
        + [jnp.zeros((item_count, -in_width % (size * LANES)), jnp.bfloat16)],
        axis=1,
    )
    in_rights = send_columns(halve_columns(d_in, size), size)
    d_input_norm, grad_norm_gain = pull_first(product_nt(d_in[:, :in_width], w_in))
    grad_input = d_middle + d_input_norm
    layer_output = (middle + live * product(act_b, w_down)).astype(jnp.bfloat16)

    model, hidden = normed_b.shape[1], act_b.shape[1]
    gu_width, width = d_gate_up.shape[1] // size, model // size
    part_rows = model // shards

    def shards_of(gradient):
        return gradient.reshape(shards, -1, gradient.shape[1])

    def folded(values):
        values = values.reshape(shards, -1, part_rows, width)
        return [values[:, i] for i in range(values.shape[1])]

    attended_end = model + attended_b.shape[1]
    branch_end = attended_end + mixed_b.shape[1]
    parts = jnp.concatenate(
        [
            shards_of(column_gradient(late, gate_up_rights, 0, model)),
            *folded(column_gradient(late, out_pair, model, model + hidden)),
            *folded(
                jnp.concatenate(
                    [
                        shards_of(column_gradient(early, branch_rights, model, attended_end)),
                        shards_of(column_gradient(early, branch_rights, attended_end, branch_end)),
                    ],
                    axis=1,
                )
            ),
        ],
        axis=2,
    )
    attended_rows = w_attn_out.shape[0]
    out_rows = attended_rows + w_mixer_out.shape[0]
    down_rows = hidden // shards

    def pair_blocks(piece):
        own = jnp.stack(send_rows(piece, size))
        return own, swap(own, "rep", size, 1)

    def write_late(place, block, outs):
        gate_up_ref, down_ref, attended_ref, mixed_ref = outs
        gate_up_ref[:, place * gu_width : (place + 1) * gu_width] = block[:, :gu_width]
        columns = slice(place * width, (place + 1) * width)
        at = gu_width
        for row in range(0, down_rows, part_rows):
            down_ref[row : row + part_rows, columns] = block[:, at : at + width]
            at += width
        for row in range(0, out_rows, part_rows):
            values = block[:, at : at + width]
            at += width
            here = max(0, min(part_rows, attended_rows - row))
            if here:
                attended_ref[row : row + here, columns] = values[:here]
            if here < part_rows:
                start = row + here - attended_rows
                mixed_ref[start : start + part_rows - here, columns] = values[here:]

    late_piece = lax.psum_scatter(parts, "shard", scatter_dimension=0, tiled=False)
    late_blocks = lax.all_gather(after(late_piece, in_rights), "rep", axis=0)
    grad_gate_up, grad_down, grad_attn_out, grad_mixer_out = unpack_columns(
        late_blocks,
        None,
        size,
        write_late,
        [
            (part_rows, d_gate_up.shape[1]),
            (down_rows, model),
            (attended_rows, model),
            (out_rows - attended_rows, model),
        ],
    )

    small = (grad_norm_gain, *d_small, grad_ffn_gain)
    flat = jnp.concatenate([part.reshape(-1) for part in small])
    flat = jnp.pad(flat, (0, -flat.shape[0] % (8 * LANES))).reshape(-1, LANES)
    flat = total_of(flat, "rep", size)
    in_rights, flat = together(in_rights, flat)
    flat = total_of(flat, "shard", shards)
    in_block = in_rights.shape[1]
    in_parts = column_gradient(early, in_rights, 0, model).reshape(shards, part_rows, in_block)

    def write_in(place, block, outs):
        start, stop = place * in_block, (place + 1) * in_block
        begin = 0
        for out_ref in outs:
            end = begin + out_ref.shape[1]
            low, high = max(start, begin), min(stop, end)
            if low < high:
                out_ref[:, low - begin : high - begin] = block[:, low - start : high - start]
            begin = end

    in_own, in_near = pair_blocks(sum_of(send_shards(in_parts, shards)))
    grad_query, grad_pair, grad_mixer_in = unpack_columns(
        in_own,
        in_near,
        size,
        write_in,
        [(part_rows, w.shape[1]) for w in (w_query, key_value_weight, w_mixer_in)],
    )
    flat = flat.reshape(-1)
    summed = []
    start = 0
    for part in small:
        summed.append(flat[start : start + part.size].reshape(part.shape))
        start += part.size
    return (
        layer_output,
        grad_input,
        summed[0],
        grad_query,
        grad_pair,
        grad_mixer_in,
        *summed[1:7],
        grad_mixer_out,
        grad_attn_out,
        summed[7],
        grad_gate_up,
        grad_down,
    )


def solution(mesh):
    return jax.shard_map(
        functools.partial(layer, mesh.shape["rep"], mesh.shape["shard"]),
        mesh=mesh,
        in_specs=(
            P(("rep", "shard"), None),
            P(("rep", "shard")),
            P(("rep", "shard"), None),
            P(),
            P("shard", None),
            P("shard", None),
            P("shard", None),
            P(),
            P(),
            P(),
            P(),
            P(),
            P(),
            P("shard", None),
            P("shard", None),
            P(),
            P("shard", None),
            P("shard", None),
        ),
        out_specs=(
            P(("rep", "shard"), None),
            P(("rep", "shard"), None),
            P(),
            P("shard", None),
            P("shard", None),
            P("shard", None),
            P(),
            P(),
            P(),
            P(),
            P(),
            P(),
            P("shard", None),
            P("shard", None),
            P(),
            P("shard", None),
            P("shard", None),
        ),
        check_vma=False,
    )
```

```python
import functools
import math

import jax
import jax.numpy as jnp
from jax import lax
from jax.experimental import pallas as pl
from jax.experimental.pallas import tpu as pltpu
from jax.sharding import PartitionSpec as P

FF = 2048
MH = 24
HEAD_SIZE = 64
NS = 128
KC = 4
QUERY_HEADS = 8
KEY_VALUE_HEADS = 2
DI = 1536
CONV = 1792


EPS = 1e-05
ROPE_BASE = 100000000000.0


def product(left, right):
    return jnp.dot(left, right, preferred_element_type=jnp.float32)


def product_tn(left, right):
    return lax.dot_general(
        left, right, (((0,), (0,)), ((), ())), preferred_element_type=jnp.float32
    )


def product_nt(left, right):
    return lax.dot_general(
        left, right, (((1,), (1,)), ((), ())), preferred_element_type=jnp.float32
    )


def rms_norm(values, gain):
    return values * lax.rsqrt(jnp.mean(values * values, axis=-1, keepdims=True) + EPS) * gain


def positions_of(segments):
    item_count = segments.shape[0]
    index = jnp.arange(item_count, dtype=jnp.int32)
    starts = jnp.concatenate([jnp.ones((1,), bool), segments[1:] != segments[:-1]])
    begin = lax.cummax(jnp.where(starts, index, 0), axis=0)
    return index - begin


def rotate(values, position):
    half = HEAD_SIZE // 2
    freqs = ROPE_BASE ** (-2.0 * jnp.arange(half, dtype=jnp.float32) / HEAD_SIZE)
    angles = position.astype(jnp.float32)[:, None] * freqs[None, :]
    cosine = jnp.cos(angles)[:, None, :]
    sine = jnp.sin(angles)[:, None, :]
    first = values[..., :half]
    second = values[..., half:]
    return jnp.concatenate(
        [first * cosine - second * sine, second * cosine + first * sine], axis=-1
    )


def silu(values):
    return values / (1.0 + jnp.exp(-values))


def attention_core(query, key_value, position, allowed):
    item_count = query.shape[0]
    heads_q = query.reshape(item_count, QUERY_HEADS, HEAD_SIZE)
    paired_items = key_value.reshape(item_count, 2, KEY_VALUE_HEADS, HEAD_SIZE)
    keys = rotate(paired_items[:, 0], position)
    values = paired_items[:, 1]
    heads_q = rotate(heads_q, position)
    shard_group = QUERY_HEADS // KEY_VALUE_HEADS
    keys = jnp.repeat(keys, shard_group, axis=1)
    values = jnp.repeat(values, shard_group, axis=1)
    scores = jnp.einsum("thd,shd->hts", heads_q, keys, precision=lax.Precision.HIGHEST) / math.sqrt(
        HEAD_SIZE
    )
    scores = jnp.where(allowed[None], scores, -jnp.inf)
    highest = jnp.max(scores, axis=-1, keepdims=True)
    expo = jnp.exp(scores - highest)
    probs = expo / jnp.sum(expo, axis=-1, keepdims=True)
    return jnp.einsum("hts,shd->thd", probs, values, precision=lax.Precision.HIGHEST).reshape(
        item_count, QUERY_HEADS * HEAD_SIZE
    )


def conv_core(conv_in, conv_weight, conv_bias, same_seg):
    item_count = conv_in.shape[0]
    total = jnp.zeros((item_count, CONV), jnp.float32) + conv_bias[None, :]
    for offset in range(KC):
        shifted = jnp.concatenate(
            [jnp.zeros((offset, CONV), jnp.float32), conv_in[: item_count - offset]], axis=0
        )
        total = total + conv_weight[KC - 1 - offset][None, :] * shifted * same_seg[offset][:, None]
    return silu(total)


def mixer_core(
    conv_out,
    gate_z,
    dt_raw,
    dt_bias,
    decay_log,
    skip_gain,
    mixer_gain,
    allowed,
):
    item_count = conv_out.shape[0]
    inner = conv_out[:, :DI].reshape(item_count, MH, HEAD_SIZE)
    bmat = conv_out[:, DI : DI + NS]
    cmat = conv_out[:, DI + NS :]
    step = jax.nn.softplus(dt_raw + dt_bias[None, :])
    csum = jnp.cumsum(step * (-jnp.exp(decay_log))[None, :], axis=0)
    gaps = csum[:, None, :] - csum[None, :, :]
    decay = jnp.exp(jnp.where(allowed[:, :, None], gaps, -jnp.inf))
    gram = jnp.dot(cmat, bmat.T, precision=lax.Precision.HIGHEST)
    mixing = gram[:, :, None] * decay * step[None, :, :]
    outputs = jnp.einsum("tsh,shp->thp", mixing, inner, precision=lax.Precision.HIGHEST)
    outputs = outputs + skip_gain[None, :, None] * inner
    gated = outputs.reshape(item_count, DI) * silu(gate_z)
    return rms_norm(gated, mixer_gain)


def swiglu(gate_up):
    return silu(gate_up[:, :FF]) * gate_up[:, FF:]


LANES = 128
SUBLANES = 8


def bit_count(size):
    return size.bit_length() - 1


def swap(values, axis_name, size, flip):
    return lax.ppermute(values, axis_name, [(i, i ^ flip) for i in range(size)])


def shift(values, axis_name, size, by):
    return lax.ppermute(values, axis_name, [(i, (i + by) % size) for i in range(size)])


def together(*values):
    return lax.optimization_barrier(values)


def after(values, done):
    return lax.optimization_barrier((values, done))[0]


def spread_first(piece, size, order):
    stacked, offsets = piece[None], [0]
    for bit in order[:-1]:
        stacked = jnp.concatenate([stacked, swap(stacked, "rep", size, 1 << bit)], axis=0)
        offsets = offsets + [offset ^ (1 << bit) for offset in offsets]
    return stacked, offsets


def spread_second(stacked, offsets, size, order):
    groups = [(stacked, offsets)]
    if order:
        flip = 1 << order[-1]
        groups.append((swap(stacked, "rep", size, flip), [offset ^ flip for offset in offsets]))
    return groups


def spread_core(groups, size):
    return groups + [
        (swap(part, "rep", size, 1), [place ^ 1 for place in places]) for part, places in groups
    ]


def spread(piece, size, order):
    return spread_core(spread_second(*spread_first(piece, size, order), size, order), size)


def assemble(shard, halves, size, shards):
    rows, width = shard.shape
    piece = rows // size
    half = piece // len(halves)

    def copies(me, own):
        yield own * rows, None, None, None, None
        for which, groups in enumerate(halves):
            for part, (_, places) in enumerate(groups):
                for slot, place in enumerate(places):
                    for step in range(1, shards):
                        owner = (own + (shards - step)) % shards
                        start = owner * rows + (me ^ place) * piece + which * half
                        yield start, which, part, slot, step - 1

    flat = [part for groups in halves for part, _ in groups]
    per_half = len(halves[0])
    if half % SUBLANES != 0:
        own = lax.axis_index("shard")
        whole = jnp.zeros((rows * shards, width), shard.dtype)
        for start, which, part, slot, step in copies(lax.axis_index("rep"), own):
            block = shard if which is None else flat[which * per_half + part][slot, step]
            whole = lax.dynamic_update_slice_in_dim(whole, block, start, axis=0)
        return whole

    def kernel(own_ref, *refs):
        *parts, whole_ref = refs
        me, own = lax.axis_index("rep"), lax.axis_index("shard")
        for start, which, part, slot, step in copies(me, own):
            start = pl.multiple_of(start, SUBLANES)
            if which is None:
                whole_ref[pl.ds(start, rows), :] = own_ref[...]
            else:
                whole_ref[pl.ds(start, half), :] = parts[which * per_half + part][slot, step]

    return pl.pallas_call(
        kernel,
        out_shape=jax.ShapeDtypeStruct((rows * shards, width), shard.dtype),
        in_specs=[pl.BlockSpec(memory_space=pltpu.VMEM)] * (1 + len(flat)),
        out_specs=pl.BlockSpec(memory_space=pltpu.VMEM),
    )(shard, *flat)


def ring_step(piece, shards):
    return shift(piece, "shard", shards, 1)


def own_piece(shard, size):
    rows = shard.shape[0] // size
    return lax.dynamic_slice_in_dim(shard, lax.axis_index("rep") * rows, rows, axis=0)


def outer_offsets(size):
    return [offset << 1 for offset in range(size // 2)]


def send_rows(rows, size):
    return [rows if offset == 0 else swap(rows, "rep", size, offset) for offset in outer_offsets(size)]


def halve_columns(rows, size):
    half = rows.shape[1] // 2
    mine = (lax.axis_index("rep") & 1) * half
    kept = lax.dynamic_slice_in_dim(rows, mine, half, axis=1)
    sent = lax.dynamic_slice_in_dim(rows, half - mine, half, axis=1)
    return jnp.stack([kept, swap(sent, "rep", size, 1)])


def send_columns(pair, size):
    width = pair.shape[2] // (size // 2)
    parts = []
    for offset in outer_offsets(size):
        target = (lax.axis_index("rep") ^ offset) >> 1
        part = lax.dynamic_slice_in_dim(pair, target * width, width, axis=2)
        parts.append(part if offset == 0 else swap(part, "rep", size, offset))
    item_count = pair.shape[1]

    def kernel(*refs):
        *part_refs, out_ref = refs
        member = lax.axis_index("rep")
        for offset, part_ref in zip(outer_offsets(size), part_refs):
            for bit in range(2):
                start = pl.multiple_of((member ^ offset ^ bit) * item_count, SUBLANES)
                out_ref[pl.ds(start, item_count), :] = part_ref[bit]

    return pl.pallas_call(
        kernel,
        out_shape=jax.ShapeDtypeStruct((size * item_count, width), pair.dtype),
        in_specs=[pl.BlockSpec(memory_space=pltpu.VMEM)] * len(parts),
        out_specs=pl.BlockSpec(memory_space=pltpu.VMEM),
    )(*parts)


def column_gradient(lefts, rights, start, stop):
    return product_tn(lefts[:, start:stop], rights).astype(jnp.bfloat16)


def send_shards(parts, shards):
    own = lax.axis_index("shard")

    def part_of(place):
        return lax.dynamic_index_in_dim(parts, place, axis=0, keepdims=False)

    return [part_of(own)] + [
        shift(part_of((own + step) % shards), "shard", shards, step) for step in range(1, shards)
    ]


def sum_of(parts):
    return sum(part.astype(jnp.float32) for part in parts).astype(jnp.bfloat16)


def unpack_columns(own, near, size, write, out_shapes):
    half = size // 2

    def kernel(*refs):
        if near is None:
            own_ref, *outs = refs
        else:
            own_ref, near_ref, *outs = refs
        member = lax.axis_index("rep")
        for place in range(size):
            if near is None:
                block = own_ref[(place % half) * 2 + place // half].astype(jnp.float32)
            else:
                slot = (member >> 1) ^ (place % half)
                same = (member & 1) == place // half
                block = jnp.where(
                    same, own_ref[slot].astype(jnp.float32), near_ref[slot].astype(jnp.float32)
                )
            write(place, block, outs)

    arrays = (own,) if near is None else (own, near)
    return pl.pallas_call(
        kernel,
        out_shape=[jax.ShapeDtypeStruct(shape, jnp.float32) for shape in out_shapes],
        in_specs=[pl.BlockSpec(memory_space=pltpu.VMEM)] * len(arrays),
        out_specs=[pl.BlockSpec(memory_space=pltpu.VMEM)] * len(out_shapes),
    )(*arrays)


def total_of(values, axis_name, size):
    for bit in range(bit_count(size)):
        values = values + swap(values, axis_name, size, 1 << bit)
    return values


def layer(
    size,
    shards,
    rows,
    segments,
    cotangent,
    norm_gain,
    w_query,
    key_value_weight,
    w_mixer_in,
    conv_weight,
    conv_bias,
    dt_bias,
    decay_log,
    skip_gain,
    mixer_gain,
    w_mixer_out,
    w_attn_out,
    ffn_gain,
    w_gate_up,
    w_down,
):
    one = list(range(1, bit_count(size)))
    two = one[::-1]
    in_shard = jnp.concatenate([w_query, key_value_weight, w_mixer_in], axis=1)
    half_in = in_shard.shape[0] // size // 2
    in_piece = jnp.concatenate(
        [own_piece(w, size) for w in (w_query, key_value_weight, w_mixer_in)], axis=1
    )
    in_pieces = []
    first_piece = in_piece
    for _ in range(1, shards):
        in_piece = ring_step(in_piece, shards)
        in_pieces.append(in_piece)
    in_pieces = jnp.stack(in_pieces)
    in_first = [
        spread_first(in_pieces[:, :half_in], size, one),
        spread_first(in_pieces[:, half_in:], size, two),
    ]
    in_second = [
        spread_second(*in_first[0], size, one),
        spread_second(*in_first[1], size, two),
    ]
    w_in = assemble(in_shard, [spread_core(groups, size) for groups in in_second], size, shards)
    model = rows.shape[1]
    blocks = w_gate_up.shape[1] // model
    rest = [own_piece(w, size) for w in (w_attn_out, w_mixer_out, w_down)]
    gate_up_piece = own_piece(w_gate_up, size)
    rest += [gate_up_piece[:, i * model : (i + 1) * model] for i in range(blocks)]
    ends = [0]
    for piece in rest:
        ends.append(ends[-1] + piece.shape[0])
    rest = lax.all_gather(after(jnp.concatenate(rest, axis=0), first_piece), ("shard", "rep"), axis=0)
    w_attn, w_mix, w_down, *gate_up_blocks = [
        rest[:, start:stop].reshape(-1, model) for start, stop in zip(ends, ends[1:])
    ]
    w_gate_up = jnp.concatenate(gate_up_blocks, axis=1)
    query_width, pair_width = w_query.shape[1], key_value_weight.shape[1]
    in_width = query_width + pair_width + w_mixer_in.shape[1]

    item_count = rows.shape[0]
    index = jnp.arange(item_count, dtype=jnp.int32)
    live = (segments >= 0).astype(jnp.float32)[:, None]
    allowed = (segments[:, None] == segments[None, :]) & (index[:, None] >= index[None, :])
    position = positions_of(segments)
    same_seg = jnp.stack(
        [
            jnp.concatenate(
                [
                    jnp.zeros((offset,), jnp.float32),
                    (segments[offset:] == segments[: item_count - offset]).astype(jnp.float32),
                ]
            )
            for offset in range(KC)
        ]
    )
    wide = rows.astype(jnp.float32)
    wide_cot = cotangent.astype(jnp.float32)
    d_out = (live * wide_cot).astype(jnp.bfloat16)
    normed, pull_first = jax.vjp(rms_norm, wide, norm_gain)
    normed_b = normed.astype(jnp.bfloat16)
    projected = product(normed_b, w_in)
    query = projected[:, :query_width]
    key_value = projected[:, query_width : query_width + pair_width]
    inner_width = mixer_gain.shape[0]
    conv_width = conv_bias.shape[0]
    pair_end = query_width + pair_width
    gate_end = pair_end + inner_width
    gate_z = projected[:, pair_end:gate_end]
    conv_in = projected[:, gate_end : gate_end + conv_width]
    dt_raw = projected[:, gate_end + conv_width :]
    out_pair = send_columns(halve_columns(d_out, size), size)
    conv_out, pull_conv = jax.vjp(
        lambda *values: conv_core(*values, same_seg), conv_in, conv_weight, conv_bias
    )

    attended, pull_attention = jax.vjp(
        lambda *values: attention_core(*values, position, allowed), query, key_value
    )
    mixed, pull_mixer = jax.vjp(
        lambda *values: mixer_core(*values, allowed),
        conv_out,
        gate_z,
        dt_raw,
        dt_bias,
        decay_log,
        skip_gain,
        mixer_gain,
    )
    attended_b = attended.astype(jnp.bfloat16)
    mixed_b = mixed.astype(jnp.bfloat16)
    middle = wide + live * (product(attended_b, w_attn) + product(mixed_b, w_mix))
    normed2, pull_second = jax.vjp(rms_norm, middle, ffn_gain)
    normed2_b = normed2.astype(jnp.bfloat16)
    gate_up = product(normed2_b, w_gate_up)
    act, pull_act = jax.vjp(swiglu, gate_up)
    act_b = act.astype(jnp.bfloat16)
    early = lax.all_gather(
        jnp.concatenate([normed_b, attended_b, mixed_b], axis=1), "rep", axis=0, tiled=True
    )
    late = lax.all_gather(jnp.concatenate([normed2_b, act_b], axis=1), "rep", axis=0, tiled=True)

    (d_gate_up,) = pull_act(product_nt(d_out, w_down))
    d_gate_up = d_gate_up.astype(jnp.bfloat16)
    gate_up_half = halve_columns(d_gate_up, size)
    d_middle_norm, grad_ffn_gain = pull_second(product_nt(d_gate_up, w_gate_up))
    d_middle = wide_cot + d_middle_norm
    d_branch = (live * d_middle).astype(jnp.bfloat16)
    branch_half = halve_columns(d_branch, size)
    d_attended = product_nt(d_branch, w_attn)
    d_mixed = product_nt(d_branch, w_mix)
    gate_up_half, branch_half, d_attended, d_mixed = together(
        gate_up_half, branch_half, d_attended, d_mixed
    )
    gate_up_rights = send_columns(gate_up_half, size)
    branch_rights = send_columns(branch_half, size)
    d_query, d_keyval = pull_attention(d_attended)
    d_attention = jnp.concatenate([d_query.astype(jnp.bfloat16), d_keyval.astype(jnp.bfloat16)], axis=1)
    gate_up_rights, branch_rights, d_attention, d_mixed = together(
        gate_up_rights, branch_rights, d_attention, d_mixed
    )
    d_conv_out, d_gate_z, d_dt_raw, *d_small = pull_mixer(d_mixed)
    late = after(late, d_conv_out)
    d_conv_in, *d_conv = pull_conv(d_conv_out)
    d_small = d_conv + d_small
    d_in = jnp.concatenate(
        [d_attention]
        + [part.astype(jnp.bfloat16) for part in (d_gate_z, d_conv_in, d_dt_raw)]
        + [jnp.zeros((item_count, -in_width % (size * LANES)), jnp.bfloat16)],
        axis=1,
    )
    in_rights = send_columns(halve_columns(d_in, size), size)
    layer_output = (middle + live * product(act_b, w_down)).astype(jnp.bfloat16)

    model, hidden = normed_b.shape[1], act_b.shape[1]
    gu_width, width = d_gate_up.shape[1] // size, model // size
    part_rows = model // shards

    def shards_of(gradient):
        return gradient.reshape(shards, -1, gradient.shape[1])

    def folded(values):
        values = values.reshape(shards, -1, part_rows, width)
        return [values[:, i] for i in range(values.shape[1])]

    attended_end = model + attended_b.shape[1]
    branch_end = attended_end + mixed_b.shape[1]
    parts = jnp.concatenate(
        [
            shards_of(column_gradient(late, gate_up_rights, 0, model)),
            *folded(column_gradient(late, out_pair, model, model + hidden)),
            *folded(
                jnp.concatenate(
                    [
                        shards_of(column_gradient(early, branch_rights, model, attended_end)),
                        shards_of(column_gradient(early, branch_rights, attended_end, branch_end)),
                    ],
                    axis=1,
                )
            ),
        ],
        axis=2,
    )
    attended_rows = w_attn_out.shape[0]
    out_rows = attended_rows + w_mixer_out.shape[0]
    down_rows = hidden // shards

    def write_late(place, block, outs):
        gate_up_ref, down_ref, attended_ref, mixed_ref = outs
        gate_up_ref[:, place * gu_width : (place + 1) * gu_width] = block[:, :gu_width]
        columns = slice(place * width, (place + 1) * width)
        at = gu_width
        for row in range(0, down_rows, part_rows):
            down_ref[row : row + part_rows, columns] = block[:, at : at + width]
            at += width
        for row in range(0, out_rows, part_rows):
            values = block[:, at : at + width]
            at += width
            here = max(0, min(part_rows, attended_rows - row))
            if here:
                attended_ref[row : row + here, columns] = values[:here]
            if here < part_rows:
                start = row + here - attended_rows
                mixed_ref[start : start + part_rows - here, columns] = values[here:]

    late_piece = lax.psum_scatter(parts, "shard", scatter_dimension=0, tiled=False)
    in_block = in_rights.shape[1]
    in_parts = column_gradient(early, in_rights, 0, model).reshape(shards, part_rows, in_block)
    in_received = send_shards(in_parts, shards)
    d_in, in_received = together(d_in, in_received)
    in_sends = send_rows(sum_of(in_received), size)
    d_normed = product_nt(d_in[:, :in_width], w_in)
    d_input_norm, grad_norm_gain = pull_first(d_normed)
    grad_input = d_middle + d_input_norm
    late_blocks = lax.all_gather(after(late_piece, in_parts), "rep", axis=0)
    grad_gate_up, grad_down, grad_attn_out, grad_mixer_out = unpack_columns(
        late_blocks,
        None,
        size,
        write_late,
        [
            (part_rows, d_gate_up.shape[1]),
            (down_rows, model),
            (attended_rows, model),
            (out_rows - attended_rows, model),
        ],
    )

    small = (grad_norm_gain, *d_small, grad_ffn_gain)
    flat = jnp.concatenate([part.reshape(-1) for part in small])
    flat = jnp.pad(flat, (0, -flat.shape[0] % (8 * LANES))).reshape(-1, LANES)
    flat = total_of(flat, "rep", size)
    in_sends, flat = together(in_sends, flat)
    in_own = jnp.stack(in_sends)
    in_near = swap(in_own, "rep", size, 1)
    flat = total_of(flat, "shard", shards)

    out_widths = [w.shape[1] for w in (w_query, key_value_weight, w_mixer_in)]

    def write_in(place, block, outs):
        start, stop = place * in_block, (place + 1) * in_block
        begin = 0
        turned = block.T
        for out_ref, out_width in zip(outs, out_widths):
            end = begin + out_width
            low, high = max(start, begin), min(stop, end)
            if low < high and out_ref.shape[0] == part_rows:
                out_ref[:, low - begin : high - begin] = block[:, low - start : high - start]
            elif low < high:
                out_ref[low - begin : high - begin, :] = turned[low - start : high - start]
            begin = end

    grad_query, grad_pair, grad_mixer_in = unpack_columns(
        in_own,
        in_near,
        size,
        write_in,
        [(part_rows, query_width), (part_rows, pair_width), (w_mixer_in.shape[1], part_rows)],
    )
    flat = flat.reshape(-1)
    summed = []
    start = 0
    for part in small:
        summed.append(flat[start : start + part.size].reshape(part.shape))
        start += part.size
    return (
        layer_output,
        grad_input,
        summed[0],
        grad_query,
        grad_pair,
        grad_mixer_in.T,
        *summed[1:7],
        grad_mixer_out,
        grad_attn_out,
        summed[7],
        grad_gate_up,
        grad_down,
    )


def solution(mesh):
    return jax.shard_map(
        functools.partial(layer, mesh.shape["rep"], mesh.shape["shard"]),
        mesh=mesh,
        in_specs=(
            P(("rep", "shard"), None),
            P(("rep", "shard")),
            P(("rep", "shard"), None),
            P(),
            P("shard", None),
            P("shard", None),
            P("shard", None),
            P(),
            P(),
            P(),
            P(),
            P(),
            P(),
            P("shard", None),
            P("shard", None),
            P(),
            P("shard", None),
            P("shard", None),
        ),
        out_specs=(
            P(("rep", "shard"), None),
            P(("rep", "shard"), None),
            P(),
            P("shard", None),
            P("shard", None),
            P("shard", None),
            P(),
            P(),
            P(),
            P(),
            P(),
            P(),
            P("shard", None),
            P("shard", None),
            P(),
            P("shard", None),
            P("shard", None),
        ),
        check_vma=False,
    )
```

```python
import functools
import math

import jax
import jax.numpy as jnp
from jax import lax
from jax.experimental import pallas as pl
from jax.experimental.pallas import tpu as pltpu
from jax.sharding import PartitionSpec as P

FF = 2048
MH = 24
HEAD_SIZE = 64
NS = 128
KC = 4
QUERY_HEADS = 8
KEY_VALUE_HEADS = 2
DI = 1536
CONV = 1792


EPS = 1e-05
ROPE_BASE = 100000000000.0


def product(left, right):
    return jnp.dot(left, right, preferred_element_type=jnp.float32)


def product_tn(left, right):
    return lax.dot_general(
        left, right, (((0,), (0,)), ((), ())), preferred_element_type=jnp.float32
    )


def product_nt(left, right):
    return lax.dot_general(
        left, right, (((1,), (1,)), ((), ())), preferred_element_type=jnp.float32
    )


def rms_norm(values, gain):
    return values * lax.rsqrt(jnp.mean(values * values, axis=-1, keepdims=True) + EPS) * gain


def positions_of(segments):
    item_count = segments.shape[0]
    index = jnp.arange(item_count, dtype=jnp.int32)
    starts = jnp.concatenate([jnp.ones((1,), bool), segments[1:] != segments[:-1]])
    begin = lax.cummax(jnp.where(starts, index, 0), axis=0)
    return index - begin


def rotate(values, position):
    half = HEAD_SIZE // 2
    freqs = ROPE_BASE ** (-2.0 * jnp.arange(half, dtype=jnp.float32) / HEAD_SIZE)
    angles = position.astype(jnp.float32)[:, None] * freqs[None, :]
    cosine = jnp.cos(angles)[:, None, :]
    sine = jnp.sin(angles)[:, None, :]
    first = values[..., :half]
    second = values[..., half:]
    return jnp.concatenate(
        [first * cosine - second * sine, second * cosine + first * sine], axis=-1
    )


def silu(values):
    return values / (1.0 + jnp.exp(-values))


def attention_core(query, key_value, position, allowed):
    item_count = query.shape[0]
    heads_q = query.reshape(item_count, QUERY_HEADS, HEAD_SIZE)
    paired_items = key_value.reshape(item_count, 2, KEY_VALUE_HEADS, HEAD_SIZE)
    keys = rotate(paired_items[:, 0], position)
    values = paired_items[:, 1]
    heads_q = rotate(heads_q, position)
    shard_group = QUERY_HEADS // KEY_VALUE_HEADS
    keys = jnp.repeat(keys, shard_group, axis=1)
    values = jnp.repeat(values, shard_group, axis=1)
    scores = jnp.einsum("thd,shd->hts", heads_q, keys, precision=lax.Precision.HIGHEST) / math.sqrt(
        HEAD_SIZE
    )
    scores = jnp.where(allowed[None], scores, -jnp.inf)
    highest = jnp.max(scores, axis=-1, keepdims=True)
    expo = jnp.exp(scores - highest)
    probs = expo / jnp.sum(expo, axis=-1, keepdims=True)
    return jnp.einsum("hts,shd->thd", probs, values, precision=lax.Precision.HIGHEST).reshape(
        item_count, QUERY_HEADS * HEAD_SIZE
    )


def conv_core(conv_in, conv_weight, conv_bias, same_seg):
    item_count = conv_in.shape[0]
    total = jnp.zeros((item_count, CONV), jnp.float32) + conv_bias[None, :]
    for offset in range(KC):
        shifted = jnp.concatenate(
            [jnp.zeros((offset, CONV), jnp.float32), conv_in[: item_count - offset]], axis=0
        )
        total = total + conv_weight[KC - 1 - offset][None, :] * shifted * same_seg[offset][:, None]
    return silu(total)


def mixer_core(
    conv_out,
    gate_z,
    dt_raw,
    dt_bias,
    decay_log,
    skip_gain,
    mixer_gain,
    allowed,
):
    item_count = conv_out.shape[0]
    inner = conv_out[:, :DI].reshape(item_count, MH, HEAD_SIZE)
    bmat = conv_out[:, DI : DI + NS]
    cmat = conv_out[:, DI + NS :]
    step = jax.nn.softplus(dt_raw + dt_bias[None, :])
    csum = jnp.cumsum(step * (-jnp.exp(decay_log))[None, :], axis=0)
    gaps = csum[:, None, :] - csum[None, :, :]
    decay = jnp.exp(jnp.where(allowed[:, :, None], gaps, -jnp.inf))
    gram = jnp.dot(cmat, bmat.T, precision=lax.Precision.HIGHEST)
    mixing = gram[:, :, None] * decay * step[None, :, :]
    outputs = jnp.einsum("tsh,shp->thp", mixing, inner, precision=lax.Precision.HIGHEST)
    outputs = outputs + skip_gain[None, :, None] * inner
    gated = outputs.reshape(item_count, DI) * silu(gate_z)
    return rms_norm(gated, mixer_gain)


def swiglu(gate_up):
    return silu(gate_up[:, :FF]) * gate_up[:, FF:]


LANES = 128
SUBLANES = 8


def bit_count(size):
    return size.bit_length() - 1


def swap(values, axis_name, size, flip):
    return lax.ppermute(values, axis_name, [(i, i ^ flip) for i in range(size)])


def shift(values, axis_name, size, by):
    return lax.ppermute(values, axis_name, [(i, (i + by) % size) for i in range(size)])


def together(*values):
    return lax.optimization_barrier(values)


def after(values, done):
    return lax.optimization_barrier((values, done))[0]


def spread_first(piece, size, order):
    stacked, offsets = piece[None], [0]
    for bit in order[:-1]:
        stacked = jnp.concatenate([stacked, swap(stacked, "rep", size, 1 << bit)], axis=0)
        offsets = offsets + [offset ^ (1 << bit) for offset in offsets]
    return stacked, offsets


def spread_second(stacked, offsets, size, order):
    groups = [(stacked, offsets)]
    if order:
        flip = 1 << order[-1]
        groups.append((swap(stacked, "rep", size, flip), [offset ^ flip for offset in offsets]))
    return groups


def spread_core(groups, size):
    return groups + [
        (swap(part, "rep", size, 1), [place ^ 1 for place in places]) for part, places in groups
    ]


def spread(piece, size, order):
    return spread_core(spread_second(*spread_first(piece, size, order), size, order), size)


def assemble(shard, halves, size, shards):
    rows, width = shard.shape
    piece = rows // size
    half = piece // len(halves)

    def copies(me, own):
        yield own * rows, None, None, None, None
        for which, groups in enumerate(halves):
            for part, (_, places) in enumerate(groups):
                for slot, place in enumerate(places):
                    for step in range(1, shards):
                        owner = (own + (shards - step)) % shards
                        start = owner * rows + (me ^ place) * piece + which * half
                        yield start, which, part, slot, step - 1

    flat = [part for groups in halves for part, _ in groups]
    per_half = len(halves[0])
    if half % SUBLANES != 0:
        own = lax.axis_index("shard")
        whole = jnp.zeros((rows * shards, width), shard.dtype)
        for start, which, part, slot, step in copies(lax.axis_index("rep"), own):
            block = shard if which is None else flat[which * per_half + part][slot, step]
            whole = lax.dynamic_update_slice_in_dim(whole, block, start, axis=0)
        return whole

    def kernel(own_ref, *refs):
        *parts, whole_ref = refs
        me, own = lax.axis_index("rep"), lax.axis_index("shard")
        for start, which, part, slot, step in copies(me, own):
            start = pl.multiple_of(start, SUBLANES)
            if which is None:
                whole_ref[pl.ds(start, rows), :] = own_ref[...]
            else:
                whole_ref[pl.ds(start, half), :] = parts[which * per_half + part][slot, step]

    return pl.pallas_call(
        kernel,
        out_shape=jax.ShapeDtypeStruct((rows * shards, width), shard.dtype),
        in_specs=[pl.BlockSpec(memory_space=pltpu.VMEM)] * (1 + len(flat)),
        out_specs=pl.BlockSpec(memory_space=pltpu.VMEM),
    )(shard, *flat)


def ring_step(piece, shards):
    return shift(piece, "shard", shards, 1)


def own_piece(shard, size):
    rows = shard.shape[0] // size
    return lax.dynamic_slice_in_dim(shard, lax.axis_index("rep") * rows, rows, axis=0)


def outer_offsets(size):
    return [offset << 1 for offset in range(size // 2)]


def send_rows(rows, size):
    return [rows if offset == 0 else swap(rows, "rep", size, offset) for offset in outer_offsets(size)]


def halve_columns(rows, size):
    half = rows.shape[1] // 2
    mine = (lax.axis_index("rep") & 1) * half
    kept = lax.dynamic_slice_in_dim(rows, mine, half, axis=1)
    sent = lax.dynamic_slice_in_dim(rows, half - mine, half, axis=1)
    return jnp.stack([kept, swap(sent, "rep", size, 1)])


def send_columns(pair, size):
    width = pair.shape[2] // (size // 2)
    parts = []
    for offset in outer_offsets(size):
        target = (lax.axis_index("rep") ^ offset) >> 1
        part = lax.dynamic_slice_in_dim(pair, target * width, width, axis=2)
        parts.append(part if offset == 0 else swap(part, "rep", size, offset))
    item_count = pair.shape[1]

    def kernel(*refs):
        *part_refs, out_ref = refs
        member = lax.axis_index("rep")
        for offset, part_ref in zip(outer_offsets(size), part_refs):
            for bit in range(2):
                start = pl.multiple_of((member ^ offset ^ bit) * item_count, SUBLANES)
                out_ref[pl.ds(start, item_count), :] = part_ref[bit]

    return pl.pallas_call(
        kernel,
        out_shape=jax.ShapeDtypeStruct((size * item_count, width), pair.dtype),
        in_specs=[pl.BlockSpec(memory_space=pltpu.VMEM)] * len(parts),
        out_specs=pl.BlockSpec(memory_space=pltpu.VMEM),
    )(*parts)


def column_gradient(lefts, rights, start, stop):
    return product_tn(lefts[:, start:stop], rights).astype(jnp.bfloat16)


def send_shards(parts, shards):
    own = lax.axis_index("shard")

    def part_of(place):
        return lax.dynamic_index_in_dim(parts, place, axis=0, keepdims=False)

    return [part_of(own)] + [
        shift(part_of((own + step) % shards), "shard", shards, step) for step in range(1, shards)
    ]


def sum_of(parts):
    return sum(part.astype(jnp.float32) for part in parts).astype(jnp.bfloat16)


def unpack_columns(own, near, size, write, out_shapes):
    half = size // 2

    def kernel(*refs):
        if near is None:
            own_ref, *outs = refs
        else:
            own_ref, near_ref, *outs = refs
        member = lax.axis_index("rep")
        for place in range(size):
            if near is None:
                block = own_ref[(place % half) * 2 + place // half].astype(jnp.float32)
            else:
                slot = (member >> 1) ^ (place % half)
                same = (member & 1) == place // half
                block = jnp.where(
                    same, own_ref[slot].astype(jnp.float32), near_ref[slot].astype(jnp.float32)
                )
            write(place, block, outs)

    arrays = (own,) if near is None else (own, near)
    return pl.pallas_call(
        kernel,
        out_shape=[jax.ShapeDtypeStruct(shape, jnp.float32) for shape in out_shapes],
        in_specs=[pl.BlockSpec(memory_space=pltpu.VMEM)] * len(arrays),
        out_specs=[pl.BlockSpec(memory_space=pltpu.VMEM)] * len(out_shapes),
    )(*arrays)


def total_of(values, axis_name, size):
    for bit in range(bit_count(size)):
        values = values + swap(values, axis_name, size, 1 << bit)
    return values


def layer(
    size,
    shards,
    rows,
    segments,
    cotangent,
    norm_gain,
    w_query,
    key_value_weight,
    w_mixer_in,
    conv_weight,
    conv_bias,
    dt_bias,
    decay_log,
    skip_gain,
    mixer_gain,
    w_mixer_out,
    w_attn_out,
    ffn_gain,
    w_gate_up,
    w_down,
):
    one = list(range(1, bit_count(size)))
    two = one[::-1]
    in_shard = jnp.concatenate([w_query, key_value_weight, w_mixer_in], axis=1)
    half_in = in_shard.shape[0] // size // 2
    in_piece = jnp.concatenate(
        [own_piece(w, size) for w in (w_query, key_value_weight, w_mixer_in)], axis=1
    )
    in_pieces = []
    first_piece = in_piece
    for _ in range(1, shards):
        in_piece = ring_step(in_piece, shards)
        in_pieces.append(in_piece)
    in_pieces = jnp.stack(in_pieces)
    in_first = [
        spread_first(in_pieces[:, :half_in], size, one),
        spread_first(in_pieces[:, half_in:], size, two),
    ]
    in_second = [
        spread_second(*in_first[0], size, one),
        spread_second(*in_first[1], size, two),
    ]
    w_in = assemble(in_shard, [spread_core(groups, size) for groups in in_second], size, shards)
    model = rows.shape[1]
    blocks = w_gate_up.shape[1] // model
    rest = [own_piece(w, size) for w in (w_attn_out, w_mixer_out, w_down)]
    gate_up_piece = own_piece(w_gate_up, size)
    rest += [gate_up_piece[:, i * model : (i + 1) * model] for i in range(blocks)]
    ends = [0]
    for piece in rest:
        ends.append(ends[-1] + piece.shape[0])
    rest = lax.all_gather(after(jnp.concatenate(rest, axis=0), first_piece), ("shard", "rep"), axis=0)
    w_attn, w_mix, w_down, *gate_up_blocks = [
        rest[:, start:stop].reshape(-1, model) for start, stop in zip(ends, ends[1:])
    ]
    w_gate_up = jnp.concatenate(gate_up_blocks, axis=1)
    query_width, pair_width = w_query.shape[1], key_value_weight.shape[1]
    in_width = query_width + pair_width + w_mixer_in.shape[1]

    item_count = rows.shape[0]
    index = jnp.arange(item_count, dtype=jnp.int32)
    live = (segments >= 0).astype(jnp.float32)[:, None]
    allowed = (segments[:, None] == segments[None, :]) & (index[:, None] >= index[None, :])
    position = positions_of(segments)
    same_seg = jnp.stack(
        [
            jnp.concatenate(
                [
                    jnp.zeros((offset,), jnp.float32),
                    (segments[offset:] == segments[: item_count - offset]).astype(jnp.float32),
                ]
            )
            for offset in range(KC)
        ]
    )
    wide = rows.astype(jnp.float32)
    wide_cot = cotangent.astype(jnp.float32)
    d_out = (live * wide_cot).astype(jnp.bfloat16)
    normed, pull_first = jax.vjp(rms_norm, wide, norm_gain)
    normed_b = normed.astype(jnp.bfloat16)
    projected = product(normed_b, w_in)
    query = projected[:, :query_width]
    key_value = projected[:, query_width : query_width + pair_width]
    inner_width = mixer_gain.shape[0]
    conv_width = conv_bias.shape[0]
    pair_end = query_width + pair_width
    gate_end = pair_end + inner_width
    gate_z = projected[:, pair_end:gate_end]
    conv_in = projected[:, gate_end : gate_end + conv_width]
    dt_raw = projected[:, gate_end + conv_width :]
    out_pair = send_columns(halve_columns(d_out, size), size)
    conv_out, pull_conv = jax.vjp(
        lambda *values: conv_core(*values, same_seg), conv_in, conv_weight, conv_bias
    )

    attended, pull_attention = jax.vjp(
        lambda *values: attention_core(*values, position, allowed), query, key_value
    )
    mixed, pull_mixer = jax.vjp(
        lambda *values: mixer_core(*values, allowed),
        conv_out,
        gate_z,
        dt_raw,
        dt_bias,
        decay_log,
        skip_gain,
        mixer_gain,
    )
    attended_b = attended.astype(jnp.bfloat16)
    mixed_b = mixed.astype(jnp.bfloat16)
    middle = wide + live * (product(attended_b, w_attn) + product(mixed_b, w_mix))
    normed2, pull_second = jax.vjp(rms_norm, middle, ffn_gain)
    normed2_b = normed2.astype(jnp.bfloat16)
    gate_up = product(normed2_b, w_gate_up)
    act, pull_act = jax.vjp(swiglu, gate_up)
    act_b = act.astype(jnp.bfloat16)
    early = lax.all_gather(
        jnp.concatenate([normed_b, attended_b, mixed_b], axis=1), "rep", axis=0, tiled=True
    )
    late = lax.all_gather(jnp.concatenate([normed2_b, act_b], axis=1), "rep", axis=0, tiled=True)

    (d_gate_up,) = pull_act(product_nt(d_out, w_down))
    d_gate_up = d_gate_up.astype(jnp.bfloat16)
    gate_up_half = halve_columns(d_gate_up, size)
    d_middle_norm, grad_ffn_gain = pull_second(product_nt(d_gate_up, w_gate_up))
    d_middle = wide_cot + d_middle_norm
    d_branch = (live * d_middle).astype(jnp.bfloat16)
    branch_half = halve_columns(d_branch, size)
    d_attended = product_nt(d_branch, w_attn)
    d_mixed = product_nt(d_branch, w_mix)
    gate_up_half, branch_half, d_attended, d_mixed = together(
        gate_up_half, branch_half, d_attended, d_mixed
    )
    gate_up_rights = send_columns(gate_up_half, size)
    branch_rights = send_columns(branch_half, size)
    d_query, d_keyval = pull_attention(d_attended)
    d_attention = jnp.concatenate([d_query.astype(jnp.bfloat16), d_keyval.astype(jnp.bfloat16)], axis=1)
    gate_up_rights, branch_rights, d_attention, d_mixed = together(
        gate_up_rights, branch_rights, d_attention, d_mixed
    )
    d_conv_out, d_gate_z, d_dt_raw, *d_small = pull_mixer(d_mixed)
    late = after(late, d_conv_out)
    d_conv_in, *d_conv = pull_conv(d_conv_out)
    d_small = d_conv + d_small
    d_in = jnp.concatenate(
        [d_attention]
        + [part.astype(jnp.bfloat16) for part in (d_gate_z, d_conv_in, d_dt_raw)]
        + [jnp.zeros((item_count, -in_width % (size * LANES)), jnp.bfloat16)],
        axis=1,
    )
    in_rights = send_columns(halve_columns(d_in, size), size)
    layer_output = (middle + live * product(act_b, w_down)).astype(jnp.bfloat16)

    model, hidden = normed_b.shape[1], act_b.shape[1]
    gu_width, width = d_gate_up.shape[1] // size, model // size
    part_rows = model // shards

    def shards_of(gradient):
        return gradient.reshape(shards, -1, gradient.shape[1])

    def folded(values):
        values = values.reshape(shards, -1, part_rows, width)
        return [values[:, i] for i in range(values.shape[1])]

    attended_end = model + attended_b.shape[1]
    branch_end = attended_end + mixed_b.shape[1]
    parts = jnp.concatenate(
        [
            shards_of(column_gradient(late, gate_up_rights, 0, model)),
            *folded(column_gradient(late, out_pair, model, model + hidden)),
            *folded(
                jnp.concatenate(
                    [
                        shards_of(column_gradient(early, branch_rights, model, attended_end)),
                        shards_of(column_gradient(early, branch_rights, attended_end, branch_end)),
                    ],
                    axis=1,
                )
            ),
        ],
        axis=2,
    )
    attended_rows = w_attn_out.shape[0]
    out_rows = attended_rows + w_mixer_out.shape[0]
    down_rows = hidden // shards

    def write_late(place, block, outs):
        gate_up_ref, down_ref, attended_ref, mixed_ref = outs
        gate_up_ref[:, place * gu_width : (place + 1) * gu_width] = block[:, :gu_width]
        columns = slice(place * width, (place + 1) * width)
        at = gu_width
        for row in range(0, down_rows, part_rows):
            down_ref[row : row + part_rows, columns] = block[:, at : at + width]
            at += width
        for row in range(0, out_rows, part_rows):
            values = block[:, at : at + width]
            at += width
            here = max(0, min(part_rows, attended_rows - row))
            if here:
                attended_ref[row : row + here, columns] = values[:here]
            if here < part_rows:
                start = row + here - attended_rows
                mixed_ref[start : start + part_rows - here, columns] = values[here:]

    late_piece = lax.psum_scatter(parts, "shard", scatter_dimension=0, tiled=False)
    in_block = in_rights.shape[1]
    d_normed = product_nt(d_in[:, :in_width], w_in)
    in_rights, d_normed = together(in_rights, d_normed)
    d_input_norm, grad_norm_gain = pull_first(d_normed)
    grad_input = d_middle + d_input_norm
    in_parts = column_gradient(early, in_rights, 0, model).reshape(shards, part_rows, in_block)
    in_received = send_shards(in_parts, shards)
    small = (grad_norm_gain, *d_small, grad_ffn_gain)
    flat = jnp.concatenate([part.reshape(-1) for part in small])
    flat = jnp.pad(flat, (0, -flat.shape[0] % (8 * LANES))).reshape(-1, LANES)
    late_blocks = lax.all_gather(after(late_piece, in_parts), "rep", axis=0)
    grad_gate_up, grad_down, grad_attn_out, grad_mixer_out = unpack_columns(
        late_blocks,
        None,
        size,
        write_late,
        [
            (part_rows, d_gate_up.shape[1]),
            (down_rows, model),
            (attended_rows, model),
            (out_rows - attended_rows, model),
        ],
    )
    in_sends = send_rows(sum_of(in_received), size)
    flat = total_of(total_of(after(flat, in_received), "rep", size), "shard", shards)
    in_own = jnp.stack(in_sends)
    in_near = swap(in_own, "rep", size, 1)
    out_widths = [w.shape[1] for w in (w_query, key_value_weight, w_mixer_in)]

    def write_in(place, block, outs):
        start, stop = place * in_block, (place + 1) * in_block
        begin = 0
        turned = block.T
        for out_ref, out_width in zip(outs, out_widths):
            end = begin + out_width
            low, high = max(start, begin), min(stop, end)
            if low < high and out_ref.shape[0] == part_rows:
                out_ref[:, low - begin : high - begin] = block[:, low - start : high - start]
            elif low < high:
                out_ref[low - begin : high - begin, :] = turned[low - start : high - start]
            begin = end

    grad_query, grad_pair, grad_mixer_in = unpack_columns(
        in_own,
        in_near,
        size,
        write_in,
        [(part_rows, query_width), (part_rows, pair_width), (w_mixer_in.shape[1], part_rows)],
    )
    flat = flat.reshape(-1)
    summed = []
    start = 0
    for part in small:
        summed.append(flat[start : start + part.size].reshape(part.shape))
        start += part.size
    return (
        layer_output,
        grad_input,
        summed[0],
        grad_query,
        grad_pair,
        grad_mixer_in.T,
        *summed[1:7],
        grad_mixer_out,
        grad_attn_out,
        summed[7],
        grad_gate_up,
        grad_down,
    )


def solution(mesh):
    return jax.shard_map(
        functools.partial(layer, mesh.shape["rep"], mesh.shape["shard"]),
        mesh=mesh,
        in_specs=(
            P(("rep", "shard"), None),
            P(("rep", "shard")),
            P(("rep", "shard"), None),
            P(),
            P("shard", None),
            P("shard", None),
            P("shard", None),
            P(),
            P(),
            P(),
            P(),
            P(),
            P(),
            P("shard", None),
            P("shard", None),
            P(),
            P("shard", None),
            P("shard", None),
        ),
        out_specs=(
            P(("rep", "shard"), None),
            P(("rep", "shard"), None),
            P(),
            P("shard", None),
            P("shard", None),
            P("shard", None),
            P(),
            P(),
            P(),
            P(),
            P(),
            P(),
            P("shard", None),
            P("shard", None),
            P(),
            P("shard", None),
            P("shard", None),
        ),
        check_vma=False,
    )
```
